32 devices in a mesh: groups: 2 (over y), region: 4 (over z), member: 2 (over x), tile: 2 (over core).
Axes of the slice: x: 2, y: 2, z: 4, core: 2. Of those that a mesh axis runs over, the one named last changes fastest.
Arguments:
- anomalies: bfloat16 [32768, 1024], P(('groups', 'region'), ('member', 'tile')), parts along dimension 0, may hold values from -12 to 12
- tapering: float32 [256, 9], P(('groups', 'region')), parts along dimension 0, may hold values from 0 to 1, as said below
Outputs:
- analysis: bfloat16 [32768, 1024], P(('groups', 'region'), ('member', 'tile')), parts along dimension 0
The draws below stay inside these ranges and needn't reach their ends.
There are 2 independent parts, one for each index of `groups`. The reference program is written for one: setup_inputs(seed, part) draws one part's arguments, and reference() takes and returns one part's arrays. A program takes and returns all parts, laid end to end along the dimension named above; each array names one. Nothing has to cross between parts.
Inputs may be any that keep to these rules, and one draw needn't show every extreme that they name: tapering[b, o + 4] is 1 at o = 0, and 0 exactly where block b + o lies outside the grid or beyond the cutoff of block b.
All inputs are finite; a program needn't handle non-finite values.
Results may differ from the reference program's by a relative error of at most 0.005.
Values may be sent and summed in bfloat16 or wider, within the bound.
No kernel may reach another device: no remote copies, remote signals or barrier semaphores. Data moves between devices by JAX's collectives and lax.ppermute only.
A program may use at most 64 MiB of HBM per device.

```python
import jax
import jax.numpy as jnp
from jax import lax

MEMBERS = 1024
BLOCK = 128
REACH = 4
SLOTS = 9
OWN_BLOCKS = 8
ALL_BLOCKS = 128
OBSERVATIONS = 16384


def draw_anomalies(key, part):
    keys = jax.random.split(key, 3)
    row_scale = jnp.exp(jax.random.uniform(keys[1], (OBSERVATIONS, 1), jnp.float32, -0.8, 0.8))
    column_scale = jnp.exp(jax.random.uniform(keys[2], (1, MEMBERS), jnp.float32, -0.8, 0.8))
    noise = jax.random.normal(keys[0], (OBSERVATIONS, MEMBERS), jnp.float32)
    values = jnp.clip(noise * row_scale * column_scale, -12.0, 12.0)
    return values.astype(jnp.bfloat16)


def draw_tapering(key, part):
    first, second = jax.random.split(key)
    stretches = ALL_BLOCKS // OWN_BLOCKS
    dense = jax.random.randint(first, (stretches,), 0, 4) == 0
    modest = jax.random.randint(second, (stretches,), 1, 3)
    level = jnp.repeat(jnp.where(dense, REACH, modest), OWN_BLOCKS, total_repeat_length=ALL_BLOCKS)
    offsets = jnp.arange(SLOTS, dtype=jnp.int32) - REACH
    blocks = jnp.arange(ALL_BLOCKS, dtype=jnp.int32)
    partner = blocks[:, None] + offsets[None, :]
    live = (jnp.abs(offsets)[None, :] <= level[:, None]) & (partner >= 0) & (partner < ALL_BLOCKS)
    half_width = 0.75 * level.astype(jnp.float32) + 0.5
    ratio = jnp.abs(offsets).astype(jnp.float32)[None, :] / half_width[:, None]
    inner = -0.25 * ratio ** 5 + 0.5 * ratio ** 4 + 0.625 * ratio ** 3 - 5.0 / 3.0 * ratio ** 2 + 1.0
    safe = jnp.maximum(ratio, 1.0)
    outer = safe ** 5 / 12.0 - 0.5 * safe ** 4 + 0.625 * safe ** 3 + 5.0 / 3.0 * safe ** 2 - 5.0 * safe + 4.0 - 2.0 / (3.0 * safe)
    value = jnp.where(ratio <= 1.0, inner, outer)
    return jnp.where(live, value, 0.0).astype(jnp.float32)


def setup_inputs(seed: int = 0, part: int = 0) -> dict:
    splits = jax.random.split(jax.random.key(seed), 3)
    part_splits = jax.random.split(jax.random.fold_in(splits[2], part), 3)
    anomalies = draw_anomalies(jax.random.fold_in(jax.random.fold_in(splits[2], part), 71), part)
    tapering = draw_tapering(jax.random.fold_in(jax.random.fold_in(splits[2], part), 71), part)
    return dict(anomalies=anomalies, tapering=tapering)


def keep_same(current):
    return current


def reference(anomalies, tapering):
    padded = jnp.pad(anomalies, ((REACH * BLOCK, REACH * BLOCK), (0, 0)))
    factor = 1.0 / (MEMBERS - 1)

    def one_block(number):
        anchor = (number + REACH) * BLOCK
        own = lax.dynamic_slice_in_dim(padded, anchor, BLOCK, 0)
        weights = lax.dynamic_index_in_dim(tapering, number, 0, keepdims=False)
        update = jnp.zeros((BLOCK, MEMBERS), jnp.float32)
        for offset in range(SLOTS):
            partner = lax.dynamic_slice_in_dim(padded, anchor + (offset - REACH) * BLOCK, BLOCK, 0)
            weight = weights[offset]

            def add_tile(current, partner=partner, weight=weight):
                covariance = lax.dot_general(own, partner, (((1,), (1,)), ((), ())), preferred_element_type=jnp.float32)
                weighted = (covariance * (weight * factor)).astype(jnp.bfloat16)
                return current + jnp.dot(weighted, partner, preferred_element_type=jnp.float32)

            update = lax.cond(weight != 0, add_tile, keep_same, update)
        return (own.astype(jnp.float32) - 0.5 * update).astype(jnp.bfloat16)

    result = lax.map(one_block, jnp.arange(ALL_BLOCKS, dtype=jnp.int32))
    return result.reshape(ALL_BLOCKS * BLOCK, MEMBERS)
```

```python
import functools

import jax
import jax.numpy as jnp
from jax import lax
from jax.experimental import pallas as pl
from jax.experimental.pallas import tpu as pltpu
from jax.sharding import PartitionSpec as P

MEMBERS = 1024
BLOCK = 128
REACH = 4
SLOTS = 9
FACTOR = 1.0 / (MEMBERS - 1)
GROUP = 4


def shifted(value, axis):
    count = lax.axis_size(axis)
    return [
        lax.ppermute(value, axis, [(i, (i + s) % count) for i in range(count)])
        for s in range(1, count)
    ]


def update_kernel(plan, parts, members, lo, count, *refs):
    arrays = 1 + max(entry[0] for entry in plan)
    taper = refs[0]
    sources = refs[1 : 1 + arrays]
    out = refs[-6]
    ybuf, wbuf, obuf, in_sem, out_sem = refs[-5:]
    copies = [
        pltpu.make_async_copy(
            sources[array].at[pl.ds(start, rows)],
            ybuf.at[part, pl.ds(to, rows)],
            in_sem.at[n],
        )
        for n, (array, part, start, to, rows) in enumerate(plan)
    ]
    for copy in copies:
        copy.start()
    for copy in copies:
        copy.wait()

    span = GROUP + 2 * REACH

    def one_group(group, carry):
        base = pl.multiple_of(group * (GROUP * BLOCK), BLOCK)
        for pair in range(0, span, 2):
            first = max(0, pair - 2 * REACH)
            last = min(GROUP, pair + 2)
            rows = (last - first) * BLOCK
            total = None
            for part in range(parts):
                left = ybuf[part, pl.ds(base + (first + REACH) * BLOCK, rows), :]
                right = ybuf[part, pl.ds(base + pair * BLOCK, 2 * BLOCK), :]
                term = lax.dot_general(
                    left, right, (((1,), (1,)), ((), ())), preferred_element_type=jnp.float32
                )
                total = term if total is None else total + term
            for i in range(GROUP):
                for half in range(2):
                    slot = pair + half - i
                    place = (
                        slice(i * BLOCK, (i + 1) * BLOCK),
                        slice((pair + half) * BLOCK, (pair + half + 1) * BLOCK),
                    )
                    if 0 <= slot < SLOTS:
                        weight = taper[lo + group * GROUP + i, slot] * FACTOR
                        tile = total[
                            (i - first) * BLOCK : (i - first + 1) * BLOCK,
                            half * BLOCK : (half + 1) * BLOCK,
                        ]
                        wbuf[place] = (tile * weight).astype(jnp.bfloat16)
                    else:
                        wbuf[place] = jnp.zeros((BLOCK, BLOCK), jnp.bfloat16)
        update = jnp.dot(
            wbuf[...],
            ybuf[0, pl.ds(base, span * BLOCK), :],
            preferred_element_type=jnp.float32,
        )
        own = ybuf[0, pl.ds(base + REACH * BLOCK, GROUP * BLOCK), :].astype(jnp.float32)
        obuf[group] = (own - 0.5 * update).astype(jnp.bfloat16)
        pltpu.make_async_copy(
            obuf.at[group],
            out.at[pl.ds(pl.multiple_of(lo * BLOCK + base, BLOCK), GROUP * BLOCK)],
            out_sem.at[group],
        ).start()
        return carry

    lax.fori_loop(0, count // GROUP, one_group, 0)
    for group in range(count // GROUP):
        pltpu.make_async_copy(
            obuf.at[group],
            out.at[pl.ds((lo + group * GROUP) * BLOCK, GROUP * BLOCK)],
            out_sem.at[group],
        ).wait()


def update_rows(taper, pieces, lo, count, previous, rows, members):
    parts = len(pieces)
    arrays, plan = [], []
    for part, held in enumerate(pieces):
        for array, first, blocks in held:
            begin = max(first, lo - REACH)
            end = min(first + blocks, lo + count + REACH)
            if begin < end:
                known = [n for n, other in enumerate(arrays) if other is array]
                if not known:
                    arrays.append(array)
                    known = [len(arrays) - 1]
                plan.append(
                    (
                        known[0],
                        part,
                        (begin - first) * BLOCK,
                        (begin - lo + REACH) * BLOCK,
                        (end - begin) * BLOCK,
                    )
                )
    operands = [taper] + arrays
    specs = [pl.BlockSpec(memory_space=pltpu.SMEM)] + [pl.BlockSpec(memory_space=pl.ANY)] * len(arrays)
    aliases = {}
    if previous is not None:
        aliases = {len(operands): 0}
        operands.append(previous)
        specs.append(pl.BlockSpec(memory_space=pl.ANY))
    window = (count + 2 * REACH) * BLOCK
    span = (GROUP + 2 * REACH) * BLOCK
    return pl.pallas_call(
        functools.partial(update_kernel, tuple(plan), parts, members, lo, count),
        out_shape=jax.ShapeDtypeStruct((rows, members), jnp.bfloat16),
        in_specs=specs,
        out_specs=pl.BlockSpec(memory_space=pl.ANY),
        input_output_aliases=aliases,
        scratch_shapes=[
            pltpu.VMEM((parts, window, members), jnp.bfloat16),
            pltpu.VMEM((GROUP * BLOCK, span), jnp.bfloat16),
            pltpu.VMEM((count // GROUP, GROUP * BLOCK, members), jnp.bfloat16),
            pltpu.SemaphoreType.DMA((len(plan),)),
            pltpu.SemaphoreType.DMA((count // GROUP,)),
        ],
        compiler_params=pltpu.CompilerParams(vmem_limit_bytes=40 * 2**20),
        cost_estimate=pl.CostEstimate(
            flops=2 * count * BLOCK * 10 * BLOCK * members * (parts + 1),
            bytes_accessed=2 * members * (parts * window + count * BLOCK),
            transcendentals=0,
        ),
    )(*operands)


def per_device(anomalies, taper):
    rows, members = anomalies.shape
    blocks = rows // BLOCK
    ring = lax.axis_size("region")
    down = [(i, i + 1) for i in range(ring - 1)]
    up = [(i + 1, i) for i in range(ring - 1)]
    halo = REACH * BLOCK

    inner = blocks - 2 * REACH
    step = inner // 3
    bounds = [0, REACH]
    while bounds[-1] < blocks - REACH:
        left = blocks - REACH - bounds[-1]
        bounds.append(bounds[-1] + (step if left > step else max(left - GROUP, GROUP) if left > GROUP else left))
    chunks = list(zip(bounds[1:-1], bounds[2:]))

    def cut(first, last):
        return lax.slice_in_dim(anomalies, first * BLOCK, last * BLOCK, axis=0)

    top, bottom = cut(0, REACH), cut(blocks - REACH, blocks)
    tops, bottoms = shifted(top, "member"), shifted(bottom, "member")
    middles = [shifted(cut(first, last), "member") for first, last in chunks]

    held = []
    own = [(anomalies, 0, blocks)]
    sets = [(own, top, bottom)]
    for s in range(len(tops)):
        listed = [(tops[s], 0, REACH)]
        for (first, last), middle in zip(chunks, middles):
            listed.append((middle[s], first, last - first))
        listed.append((bottoms[s], blocks - REACH, REACH))
        sets.append((listed, tops[s], bottoms[s]))
    for listed, head, tail in sets:
        before = (lax.ppermute(tail, "region", down), -REACH, REACH)
        after = (lax.ppermute(head, "region", up), blocks, REACH)
        held.append([before] + listed + [after])

    seen = {}
    pieces = list(held)
    for turn in range(lax.axis_size("tile") - 1):
        for listed in held:
            pieces.append(
                [(shifted(array, "tile")[turn], first, count) for array, first, count in listed]
            )

    result = None
    edges = [last for _, last in chunks]
    lo = 0
    for n, last in enumerate(edges):
        hi = blocks if n == len(edges) - 1 else (last - REACH) // GROUP * GROUP
        if hi > lo:
            result = update_rows(taper, pieces, lo, hi - lo, result, rows, members)
            lo = hi
    return result


def solution(mesh):
    in_specs = (P(("groups", "region"), ("member", "tile")), P(("groups", "region"), None))
    out_specs = P(("groups", "region"), ("member", "tile"))
    return jax.shard_map(
        per_device, mesh=mesh, in_specs=in_specs, out_specs=out_specs, check_vma=False
    )
```

```python
import functools

import jax
import jax.numpy as jnp
from jax import lax
from jax.experimental import pallas as pl
from jax.experimental.pallas import tpu as pltpu
from jax.sharding import PartitionSpec as P


MEMBERS = 1024
BLOCK = 128
REACH = 4
SLOTS = 9
FACTOR = 1.0 / (MEMBERS - 1)
PAIR = 2
ROWS = PAIR * BLOCK
NEAR = REACH // PAIR


def shifted(value, axis):
    count = lax.axis_size(axis)
    return [
        lax.ppermute(value, axis, [(i, (i + s) % count) for i in range(count)])
        for s in range(1, count)
    ]


def tile_rows(start, count=1):
    return pl.ds(start * ROWS, count * ROWS)


def update_kernel(job, *refs):
    slots, parts = job["slots"], job["parts"]
    plan, steps, owned = job["plan"], job["steps"], job["owned"]
    acc_in, acc_out, finished = job["acc_in"], job["acc_out"], job["finished"]
    arrays = job["arrays"]
    taper = refs[0]
    sources = refs[1 : 1 + arrays]
    inputs = refs[1 + arrays : 1 + arrays + len(acc_in)]
    outs = refs[1 + arrays + len(acc_in) + job["aliased"] :]
    if finished:
        out, outs = outs[0], outs[1:]
    carried, outs = outs[: len(acc_out)], outs[len(acc_out) :]
    ybuf, acc, wcol, wrow, obuf, in_sem, acc_sem, out_sem = outs

    def fetch(n):
        array, part, start, slot = plan[n]
        return pltpu.make_async_copy(
            sources[array].at[tile_rows(start)], ybuf.at[part, slot], in_sem.at[n]
        )

    def take(n):
        return pltpu.make_async_copy(inputs[n], acc.at[slots[acc_in[n]]], acc_sem.at[n])

    for n in range(len(plan)):
        fetch(n).start()
    for n in range(len(acc_in)):
        take(n).start()
    here, begun = set(), set()

    def arrive(pair):
        if pair not in here:
            here.add(pair)
            for n in range(len(plan)):
                if plan[n][3] == slots[pair]:
                    fetch(n).wait()

    def add(pair, value):
        slot = slots[pair]
        if pair in begun:
            acc[slot] = acc[slot] + value
        elif pair in acc_in:
            take(acc_in.index(pair)).wait()
            acc[slot] = acc[slot] + value
        else:
            acc[slot] = value
        begun.add(pair)

    def weighted(c, i_pair, j_pair, base, flip):
        rows = []
        for ii in range(PAIR):
            row = []
            for jj in range(PAIR):
                i, j = i_pair * PAIR + ii, j_pair * PAIR + jj
                slot = (i - j if flip else j - i) + REACH
                if 0 <= slot < SLOTS:
                    weight = taper[j if flip else i, slot] * FACTOR
                    tile = c[
                        base + ii * BLOCK : base + (ii + 1) * BLOCK,
                        jj * BLOCK : (jj + 1) * BLOCK,
                    ]
                    row.append((tile * weight).astype(jnp.bfloat16))
                else:
                    row.append(jnp.zeros((BLOCK, BLOCK), jnp.bfloat16))
            rows.append(jnp.concatenate(row, axis=1))
        return jnp.concatenate(rows, axis=0)

    for j, first, count in steps:
        near = list(range(first, first + count))
        for pair in near + [j]:
            arrive(pair)
        total = None
        for part in range(parts):
            left = ybuf[part, pl.ds(slots[first], count)].reshape(count * ROWS, -1)
            term = lax.dot_general(
                left,
                ybuf[part, slots[j]],
                (((1,), (1,)), ((), ())),
                preferred_element_type=jnp.float32,
            )
            total = term if total is None else total + term
        others = [i for i in near if i != j]
        for k, i in enumerate(near):
            if i in owned:
                wcol[tile_rows(k)] = weighted(total, i, j, k * ROWS, False)
            if j in owned and i != j:
                wrow[tile_rows(others.index(i))] = weighted(total, i, j, k * ROWS, True)
        for k, i in enumerate(near):
            if i in owned:
                add(
                    i,
                    jnp.dot(
                        wcol[tile_rows(k)],
                        ybuf[0, slots[j]],
                        preferred_element_type=jnp.float32,
                    ),
                )
        if j in owned and others:
            value = None
            for k, i in enumerate(others):
                term = lax.dot_general(
                    wrow[tile_rows(k)],
                    ybuf[0, slots[i]],
                    (((0,), (0,)), ((), ())),
                    preferred_element_type=jnp.float32,
                )
                value = term if value is None else value + term
            add(j, value)

    def store(n):
        return pltpu.make_async_copy(
            obuf.at[n], out.at[tile_rows(finished[n])], out_sem.at[n]
        )

    def hand_on(n):
        return pltpu.make_async_copy(
            acc.at[slots[acc_out[n]]], carried[n], out_sem.at[len(finished) + n]
        )

    for n, pair in enumerate(acc_out):
        if pair in acc_in and pair not in begun:
            take(acc_in.index(pair)).wait()
        hand_on(n).start()
    for n, pair in enumerate(finished):
        if pair in acc_in and pair not in begun:
            take(acc_in.index(pair)).wait()
        own = ybuf[0, slots[pair]].astype(jnp.float32)
        obuf[n] = (own - 0.5 * acc[slots[pair]]).astype(jnp.bfloat16)
        store(n).start()
    for n in range(len(acc_out)):
        hand_on(n).wait()
    for n in range(len(finished)):
        store(n).wait()


def run_steps(taper, pieces, steps, owned, state, finished, result, rows, members):
    parts = len(pieces)
    needed = set()
    for j, first, count in steps:
        needed |= {j} | set(range(first, first + count))
    needed |= set(finished)
    slots = {pair: n for n, pair in enumerate(sorted(needed))}
    touched = set()
    for j, first, count in steps:
        near = set(range(first, first + count))
        touched |= near & owned
        if j in owned and near - {j}:
            touched.add(j)
    acc_in = [pair for pair in sorted(touched | set(finished)) if pair in state]
    acc_out = sorted(touched - set(finished))
    order = []
    for j, first, count in steps:
        for pair in [j] + list(range(first, first + count)):
            if pair not in order:
                order.append(pair)
    order += [pair for pair in finished if pair not in order]
    arrays, plan = [], []
    for pair in order:
        for part in range(parts):
            array, start = pieces[part][pair]
            known = [n for n, other in enumerate(arrays) if other is array]
            if not known:
                arrays.append(array)
                known = [len(arrays) - 1]
            plan.append((known[0], part, start, slots[pair]))
    aliased = int(bool(finished) and result is not None)
    job = dict(
        slots=slots, parts=parts, plan=plan, steps=steps, owned=owned, acc_in=acc_in,
        acc_out=acc_out, finished=finished, arrays=len(arrays), aliased=aliased,
    )
    operands = [taper] + arrays + [state[pair] for pair in acc_in]
    anywhere = pl.BlockSpec(memory_space=pl.ANY)
    specs = [pl.BlockSpec(memory_space=pltpu.SMEM)] + [anywhere] * (len(operands) - 1)
    aliases = {}
    shapes = []
    if finished:
        shapes.append(jax.ShapeDtypeStruct((rows, members), jnp.bfloat16))
        if aliased:
            aliases = {len(operands): 0}
            operands.append(result)
            specs.append(anywhere)
    shapes += [jax.ShapeDtypeStruct((ROWS, members), jnp.float32)] * len(acc_out)
    widest = max(count for _, _, count in steps)
    count = len(needed)
    products = sum(n for _, _, n in steps)
    outputs = pl.pallas_call(
        functools.partial(update_kernel, job),
        out_shape=shapes,
        in_specs=specs,
        out_specs=[anywhere] * len(shapes),
        input_output_aliases=aliases,
        scratch_shapes=[
            pltpu.VMEM((parts, count, ROWS, members), jnp.bfloat16),
            pltpu.VMEM((count, ROWS, members), jnp.float32),
            pltpu.VMEM((widest * ROWS, ROWS), jnp.bfloat16),
            pltpu.VMEM((widest * ROWS, ROWS), jnp.bfloat16),
            pltpu.VMEM((max(len(finished), 1), ROWS, members), jnp.bfloat16),
            pltpu.SemaphoreType.DMA((len(plan),)),
            pltpu.SemaphoreType.DMA((max(len(acc_in), 1),)),
            pltpu.SemaphoreType.DMA((len(finished) + len(acc_out),)),
        ],
        compiler_params=pltpu.CompilerParams(vmem_limit_bytes=32 * 2**20),
        cost_estimate=pl.CostEstimate(
            flops=2 * products * ROWS * ROWS * members * (parts + 2),
            bytes_accessed=2 * ROWS * members * (len(plan) + 3 * len(finished)),
            transcendentals=0,
        ),
    )(*operands)
    if finished:
        result, outputs = outputs[0], outputs[1:]
    state = {pair: value for pair, value in state.items() if pair not in touched}
    state.update(zip(acc_out, outputs))
    for pair in finished:
        state.pop(pair, None)
    return result, state


def chunk_bounds(pairs):
    first, last = NEAR, pairs - NEAR
    tail = [2, 2]
    bulk = last - first - sum(tail)
    sizes = [(bulk + 1) // 2, bulk // 2] + tail
    bounds = [first]
    for size in sizes:
        if size:
            bounds.append(bounds[-1] + size)
    return list(zip(bounds, bounds[1:]))


def per_device(anomalies, taper):
    rows, members = anomalies.shape
    pairs = rows // ROWS
    ring = lax.axis_size("region")
    down = [(i, i + 1) for i in range(ring - 1)]
    up = [(i + 1, i) for i in range(ring - 1)]
    chunks = chunk_bounds(pairs)

    def cut(first, last):
        return lax.slice_in_dim(anomalies, first * ROWS, last * ROWS, axis=0)

    top, bottom = cut(0, NEAR), cut(pairs - NEAR, pairs)
    tops = shifted(top, "member")
    bottoms = shifted(bottom, "member")
    middles = []
    for first, last in chunks:
        middles.append(shifted(cut(first, last), "member"))

    sets = [([(anomalies, 0, pairs)], top, bottom)]
    for s in range(len(tops)):
        listed = [(tops[s], 0, NEAR)]
        for (first, last), middle in zip(chunks, middles):
            listed.append((middle[s], first, last - first))
        listed.append((bottoms[s], pairs - NEAR, NEAR))
        sets.append((listed, tops[s], bottoms[s]))
    held = []
    for listed, head, tail in sets:
        before = (lax.ppermute(tail, "region", down), -NEAR, NEAR)
        after = (lax.ppermute(head, "region", up), pairs, NEAR)
        held.append([before, after] + listed)
    for turn in range(lax.axis_size("tile") - 1):
        held += [
            [(shifted(array, "tile")[turn], first, count) for array, first, count in listed]
            for listed in list(held)
        ]
    pieces = [
        {first + n: (array, n) for array, first, count in listed for n in range(count)}
        for listed in held
    ]

    owned = set(range(pairs))
    state, result = {}, None

    def steps_for(fresh, before):
        there, steps = set(before), []
        for j in fresh:
            there.add(j)
            near = [i for i in range(j - NEAR, j + NEAR + 1) if i in there and (i in owned or j in owned)]
            while near:
                run = [near[0]]
                while run[-1] + 1 in near:
                    run.append(run[-1] + 1)
                steps.append((j, run[0], len(run)))
                near = near[len(run) :]
        return steps, there

    low = list(range(-NEAR, NEAR))
    high = list(range(pairs - NEAR, pairs + NEAR))
    there, done = set(), set()
    batches = [high, low + list(range(*chunks[0]))] + [list(range(*c)) for c in chunks[1:]]
    for fresh in batches:
        steps, there = steps_for(fresh, there)
        ready = [
            i for i in range(pairs)
            if i not in done and all(k in there for k in range(i - NEAR, i + NEAR + 1))
        ]
        done |= set(ready)
        result, state = run_steps(taper, pieces, steps, owned, state, ready, result, rows, members)
    return result


def solution(mesh):
    in_specs = (P(("groups", "region"), ("member", "tile")), P(("groups", "region"), None))
    out_specs = P(("groups", "region"), ("member", "tile"))

    return jax.shard_map(
        per_device, mesh=mesh, in_specs=in_specs, out_specs=out_specs, check_vma=False
    )
```

```python
import functools

import jax
import jax.numpy as jnp
from jax import lax
from jax.experimental import pallas as pl
from jax.experimental.pallas import tpu as pltpu
from jax.sharding import PartitionSpec as P


MEMBERS = 1024
BLOCK = 128
REACH = 4
SLOTS = 9
FACTOR = 1.0 / (MEMBERS - 1)
PAIR = 2
ROWS = PAIR * BLOCK
NEAR = REACH // PAIR


def shifted(value, axis):
    count = lax.axis_size(axis)
    return [
        lax.ppermute(value, axis, [(i, (i + s) % count) for i in range(count)])
        for s in range(1, count)
    ]


def tile_rows(start, count=1):
    return pl.ds(start * ROWS, count * ROWS)


def update_kernel(job, *refs):
    slots = job["slots"]
    plan, steps, owned = job["plan"], job["steps"], job["owned"]
    acc_in, acc_out, finished = job["acc_in"], job["acc_out"], job["finished"]
    arrays, members = job["arrays"], job["members"]
    taper = refs[0]
    sources = refs[1 : 1 + arrays]
    inputs = refs[1 + arrays : 1 + arrays + len(acc_in)]
    outs = refs[1 + arrays + len(acc_in) + job["aliased"] :]
    if finished:
        out, outs = outs[0], outs[1:]
    carried, outs = outs[: len(acc_out)], outs[len(acc_out) :]
    ybuf, acc, obuf, in_sem, acc_sem, out_sem = outs

    def fetch(n):
        array, part, start, slot = plan[n]
        return pltpu.make_async_copy(
            sources[array].at[tile_rows(start)],
            ybuf.at[slot, :, pl.ds(part * members, members)],
            in_sem.at[n],
        )

    def take(n):
        return pltpu.make_async_copy(inputs[n], acc.at[slots[acc_in[n]]], acc_sem.at[n])

    for n in range(len(plan)):
        fetch(n).start()
    for n in range(len(acc_in)):
        take(n).start()
    here, begun = set(), set()

    def arrive(pair):
        if pair not in here:
            here.add(pair)
            for n in range(len(plan)):
                if plan[n][3] == slots[pair]:
                    fetch(n).wait()

    def add(pair, value):
        slot = slots[pair]
        if pair in begun:
            acc[slot] = acc[slot] + value
        elif pair in acc_in:
            take(acc_in.index(pair)).wait()
            acc[slot] = acc[slot] + value
        else:
            acc[slot] = value
        begun.add(pair)

    def own(pair):
        return ybuf[slots[pair], :, :members]

    def weighted(c, i_pair, j_pair, flip):
        rows = []
        for ii in range(PAIR):
            row = []
            for jj in range(PAIR):
                i, j = i_pair * PAIR + ii, j_pair * PAIR + jj
                slot = (i - j if flip else j - i) + REACH
                if 0 <= slot < SLOTS:
                    weight = taper[j if flip else i, slot] * FACTOR
                    tile = c[ii * BLOCK : (ii + 1) * BLOCK, jj * BLOCK : (jj + 1) * BLOCK]
                    row.append((tile * weight).astype(jnp.bfloat16))
                else:
                    row.append(jnp.zeros((BLOCK, BLOCK), jnp.bfloat16))
            rows.append(jnp.concatenate(row, axis=1))
        return jnp.concatenate(rows, axis=0)

    for j, first, count in steps:
        near = list(range(first, first + count))
        for pair in [j] + near:
            arrive(pair)
        gram = lax.dot_general(
            ybuf[pl.ds(slots[first], count)].reshape(count * ROWS, -1),
            ybuf[slots[j]],
            (((1,), (1,)), ((), ())),
            preferred_element_type=jnp.float32,
        )
        tiles = {i: gram[n * ROWS : (n + 1) * ROWS] for n, i in enumerate(near)}
        mine = [i for i in near if i in owned]
        if mine:
            value = jnp.dot(
                jnp.concatenate([weighted(tiles[i], i, j, False) for i in mine], axis=0),
                own(j),
                preferred_element_type=jnp.float32,
            )
            for n, i in enumerate(mine):
                add(i, value[n * ROWS : (n + 1) * ROWS])
        others = [i for i in near if i != j]
        if j in owned and others:
            value = None
            for i in others:
                term = jnp.dot(
                    weighted(tiles[i], i, j, True).T, own(i), preferred_element_type=jnp.float32
                )
                value = term if value is None else value + term
            add(j, value)

    def store(n):
        return pltpu.make_async_copy(
            obuf.at[n], out.at[tile_rows(finished[n])], out_sem.at[n]
        )

    def hand_on(n):
        return pltpu.make_async_copy(
            acc.at[slots[acc_out[n]]], carried[n], out_sem.at[len(finished) + n]
        )

    for n, pair in enumerate(acc_out):
        if pair in acc_in and pair not in begun:
            take(acc_in.index(pair)).wait()
        hand_on(n).start()
    for n, pair in enumerate(finished):
        if pair in acc_in and pair not in begun:
            take(acc_in.index(pair)).wait()
        obuf[n] = (own(pair).astype(jnp.float32) - 0.5 * acc[slots[pair]]).astype(jnp.bfloat16)
        store(n).start()
    for n in range(len(acc_out)):
        hand_on(n).wait()
    for n in range(len(finished)):
        store(n).wait()


def run_steps(taper, pieces, steps, owned, state, finished, result, rows, members):
    parts = len(pieces)
    needed = set()
    for j, first, count in steps:
        needed |= {j} | set(range(first, first + count))
    needed |= set(finished)
    slots = {pair: n for n, pair in enumerate(sorted(needed))}
    touched = set()
    for j, first, count in steps:
        near = set(range(first, first + count))
        touched |= near & owned
        if j in owned and near - {j}:
            touched.add(j)
    acc_in = [pair for pair in sorted(touched | set(finished)) if pair in state]
    acc_out = sorted(touched - set(finished))
    order = []
    for j, first, count in steps:
        for pair in [j] + list(range(first, first + count)):
            if pair not in order:
                order.append(pair)
    order += [pair for pair in finished if pair not in order]
    arrays, plan = [], []
    for pair in order:
        for part in range(parts):
            array, start = pieces[part][pair]
            known = [n for n, other in enumerate(arrays) if other is array]
            if not known:
                arrays.append(array)
                known = [len(arrays) - 1]
            plan.append((known[0], part, start, slots[pair]))
    aliased = int(bool(finished) and result is not None)
    job = dict(
        slots=slots, parts=parts, plan=plan, steps=steps, owned=owned, acc_in=acc_in,
        acc_out=acc_out, finished=finished, arrays=len(arrays), aliased=aliased,
        members=members,
    )
    operands = [taper] + arrays + [state[pair] for pair in acc_in]
    anywhere = pl.BlockSpec(memory_space=pl.ANY)
    specs = [pl.BlockSpec(memory_space=pltpu.SMEM)] + [anywhere] * (len(operands) - 1)
    aliases = {}
    shapes = []
    if finished:
        shapes.append(jax.ShapeDtypeStruct((rows, members), jnp.bfloat16))
        if aliased:
            aliases = {len(operands): 0}
            operands.append(result)
            specs.append(anywhere)
    shapes += [jax.ShapeDtypeStruct((ROWS, members), jnp.float32)] * len(acc_out)
    count = len(needed)
    products = sum(n for _, _, n in steps)
    outputs = pl.pallas_call(
        functools.partial(update_kernel, job),
        out_shape=shapes,
        in_specs=specs,
        out_specs=[anywhere] * len(shapes),
        input_output_aliases=aliases,
        scratch_shapes=[
            pltpu.VMEM((count, ROWS, parts * members), jnp.bfloat16),
            pltpu.VMEM((count, ROWS, members), jnp.float32),
            pltpu.VMEM((max(len(finished), 1), ROWS, members), jnp.bfloat16),
            pltpu.SemaphoreType.DMA((len(plan),)),
            pltpu.SemaphoreType.DMA((max(len(acc_in), 1),)),
            pltpu.SemaphoreType.DMA((len(finished) + len(acc_out),)),
        ],
        compiler_params=pltpu.CompilerParams(vmem_limit_bytes=32 * 2**20),
        cost_estimate=pl.CostEstimate(
            flops=2 * products * ROWS * ROWS * members * (parts + 2),
            bytes_accessed=2 * ROWS * members * (len(plan) + 3 * len(finished)),
            transcendentals=0,
        ),
    )(*operands)
    if finished:
        result, outputs = outputs[0], outputs[1:]
    state = {pair: value for pair, value in state.items() if pair not in touched}
    state.update(zip(acc_out, outputs))
    for pair in finished:
        state.pop(pair, None)
    return result, state


def chunk_bounds(pairs):
    first, last = NEAR, pairs - NEAR
    tail = [2, 2]
    bulk = last - first - sum(tail)
    sizes = [(bulk + 1) // 2, bulk // 2] + tail
    bounds = [first]
    for size in sizes:
        if size:
            bounds.append(bounds[-1] + size)
    return list(zip(bounds, bounds[1:]))


def per_device(anomalies, taper):
    rows, members = anomalies.shape
    pairs = rows // ROWS
    ring = lax.axis_size("region")
    down = [(i, i + 1) for i in range(ring - 1)]
    up = [(i + 1, i) for i in range(ring - 1)]
    chunks = chunk_bounds(pairs)

    def cut(first, last):
        return lax.slice_in_dim(anomalies, first * ROWS, last * ROWS, axis=0)

    top, bottom = cut(0, NEAR), cut(pairs - NEAR, pairs)
    tops = shifted(top, "member")
    bottoms = shifted(bottom, "member")
    middles = []
    for first, last in chunks:
        middles.append(shifted(cut(first, last), "member"))

    sets = [([(anomalies, 0, pairs)], top, bottom)]
    for s in range(len(tops)):
        listed = [(tops[s], 0, NEAR)]
        for (first, last), middle in zip(chunks, middles):
            listed.append((middle[s], first, last - first))
        listed.append((bottoms[s], pairs - NEAR, NEAR))
        sets.append((listed, tops[s], bottoms[s]))
    held = []
    for listed, head, tail in sets:
        before = (lax.ppermute(tail, "region", down), -NEAR, NEAR)
        after = (lax.ppermute(head, "region", up), pairs, NEAR)
        held.append([before, after] + listed)
    for turn in range(lax.axis_size("tile") - 1):
        held += [
            [(shifted(array, "tile")[turn], first, count) for array, first, count in listed]
            for listed in list(held)
        ]
    pieces = [
        {first + n: (array, n) for array, first, count in listed for n in range(count)}
        for listed in held
    ]

    owned = set(range(pairs))
    state, result = {}, None

    def steps_for(fresh, before):
        there, steps = set(before), []
        for j in fresh:
            there.add(j)
            near = [i for i in range(j - NEAR, j + NEAR + 1) if i in there and (i in owned or j in owned)]
            while near:
                run = [near[0]]
                while run[-1] + 1 in near:
                    run.append(run[-1] + 1)
                steps.append((j, run[0], len(run)))
                near = near[len(run) :]
        return steps, there

    low = list(range(-NEAR, NEAR))
    high = list(range(pairs - NEAR, pairs + NEAR))
    there, done = set(), set()
    batches = [high, low + list(range(*chunks[0]))] + [list(range(*c)) for c in chunks[1:]]
    for fresh in batches:
        steps, there = steps_for(fresh, there)
        ready = [
            i for i in range(pairs)
            if i not in done and all(k in there for k in range(i - NEAR, i + NEAR + 1))
        ]
        done |= set(ready)
        result, state = run_steps(taper, pieces, steps, owned, state, ready, result, rows, members)
    return result


def solution(mesh):
    in_specs = (P(("groups", "region"), ("member", "tile")), P(("groups", "region"), None))
    out_specs = P(("groups", "region"), ("member", "tile"))

    return jax.shard_map(
        per_device, mesh=mesh, in_specs=in_specs, out_specs=out_specs, check_vma=False
    )
```

```python
import functools

import jax
import jax.numpy as jnp
from jax import lax
from jax.experimental import pallas as pl
from jax.experimental.pallas import tpu as pltpu
from jax.sharding import PartitionSpec as P


MEMBERS = 1024
BLOCK = 128
REACH = 4
SLOTS = 9
FACTOR = 1.0 / (MEMBERS - 1)
PAIR = 2
ROWS = PAIR * BLOCK
NEAR = REACH // PAIR


def shifted(value, axis):
    count = lax.axis_size(axis)
    return [
        lax.ppermute(value, axis, [(i, (i + s) % count) for i in range(count)])
        for s in range(1, count)
    ]


def tile_rows(start, count=1):
    return pl.ds(start * ROWS, count * ROWS)


def update_kernel(job, *refs):
    parts = job["parts"]
    plan, steps, owned = job["plan"], job["steps"], job["owned"]
    acc_in, acc_out, finished = job["acc_in"], job["acc_out"], job["finished"]
    arrays = job["arrays"]
    taper = refs[0]
    sources = refs[1 : 1 + arrays]
    inputs = dict(zip(acc_in, refs[1 + arrays : 1 + arrays + len(acc_in)]))
    outs = refs[1 + arrays + len(acc_in) + job["aliased"] :]
    if finished:
        out, outs = outs[0], outs[1:]
    carried, outs = outs[: len(acc_out)], outs[len(acc_out) :]
    acc, obuf, out_sem = outs
    sums = {pair: carried[n] for n, pair in enumerate(acc_out)}
    sums |= {pair: acc.at[n] for n, pair in enumerate(finished)}
    begun = set()

    def piece(pair, part):
        array, start = plan[pair, part]
        return sources[array][tile_rows(start), :]

    def held(pair):
        return jnp.concatenate([piece(pair, part) for part in range(parts)], axis=1)

    def own(pair):
        return piece(pair, 0)

    def add(pair, value):
        if pair in begun:
            value = sums[pair][...] + value
        elif pair in acc_in:
            value = inputs[pair][...] + value
        sums[pair][...] = value
        begun.add(pair)

    def weighted(c, i_pair, j_pair, flip):
        rows = []
        for ii in range(PAIR):
            row = []
            for jj in range(PAIR):
                i, j = i_pair * PAIR + ii, j_pair * PAIR + jj
                slot = (i - j if flip else j - i) + REACH
                if 0 <= slot < SLOTS:
                    weight = taper[j if flip else i, slot] * FACTOR
                    tile = c[ii * BLOCK : (ii + 1) * BLOCK, jj * BLOCK : (jj + 1) * BLOCK]
                    row.append((tile * weight).astype(jnp.bfloat16))
                else:
                    row.append(jnp.zeros((BLOCK, BLOCK), jnp.bfloat16))
            rows.append(jnp.concatenate(row, axis=1))
        return jnp.concatenate(rows, axis=0)

    for j, first, count in steps:
        near = list(range(first, first + count))
        gram = lax.dot_general(
            jnp.concatenate([held(i) for i in near], axis=0),
            held(j),
            (((1,), (1,)), ((), ())),
            preferred_element_type=jnp.float32,
        )
        tiles = {i: gram[n * ROWS : (n + 1) * ROWS] for n, i in enumerate(near)}
        mine = [i for i in near if i in owned]
        if mine:
            value = jnp.dot(
                jnp.concatenate([weighted(tiles[i], i, j, False) for i in mine], axis=0),
                own(j),
                preferred_element_type=jnp.float32,
            )
            for n, i in enumerate(mine):
                add(i, value[n * ROWS : (n + 1) * ROWS])
        others = [i for i in near if i != j]
        if j in owned and others:
            value = None
            for i in others:
                term = jnp.dot(
                    weighted(tiles[i], i, j, True).T, own(i), preferred_element_type=jnp.float32
                )
                value = term if value is None else value + term
            add(j, value)

    def store(n):
        return pltpu.make_async_copy(
            obuf.at[n], out.at[tile_rows(finished[n])], out_sem.at[n]
        )

    for n, pair in enumerate(finished):
        update = (sums if pair in begun else inputs)[pair][...]
        obuf[n] = (own(pair).astype(jnp.float32) - 0.5 * update).astype(jnp.bfloat16)
        store(n).start()
    for n in range(len(finished)):
        store(n).wait()


def run_steps(taper, pieces, steps, owned, state, finished, result, rows, members):
    parts = len(pieces)
    needed = set()
    for j, first, count in steps:
        needed |= {j} | set(range(first, first + count))
    needed |= set(finished)
    touched = set()
    for j, first, count in steps:
        near = set(range(first, first + count))
        touched |= near & owned
        if j in owned and near - {j}:
            touched.add(j)
    acc_in = [pair for pair in sorted(touched | set(finished)) if pair in state]
    acc_out = sorted(touched - set(finished))
    arrays, plan = [], {}
    for pair in sorted(needed):
        for part in range(parts):
            array, start = pieces[part][pair]
            known = [n for n, other in enumerate(arrays) if other is array]
            if not known:
                arrays.append(array)
                known = [len(arrays) - 1]
            plan[pair, part] = (known[0], start)
    aliased = int(bool(finished) and result is not None)
    job = dict(
        parts=parts, plan=plan, steps=steps, owned=owned, acc_in=acc_in,
        acc_out=acc_out, finished=finished, arrays=len(arrays), aliased=aliased,
    )
    operands = [taper] + arrays + [state[pair] for pair in acc_in]
    anywhere = pl.BlockSpec(memory_space=pl.ANY)
    inside = pl.BlockSpec(memory_space=pltpu.VMEM)
    specs = [pl.BlockSpec(memory_space=pltpu.SMEM)] + [inside] * (len(operands) - 1)
    aliases = {}
    shapes = []
    if finished:
        shapes.append(jax.ShapeDtypeStruct((rows, members), jnp.bfloat16))
        if aliased:
            aliases = {len(operands): 0}
            operands.append(result)
            specs.append(anywhere)
    shapes += [jax.ShapeDtypeStruct((ROWS, members), jnp.float32)] * len(acc_out)
    products = sum(n for _, _, n in steps)
    outputs = pl.pallas_call(
        functools.partial(update_kernel, job),
        out_shape=shapes,
        in_specs=specs,
        out_specs=[anywhere] * int(bool(finished)) + [inside] * len(acc_out),
        input_output_aliases=aliases,
        scratch_shapes=[
            pltpu.VMEM((max(len(finished), 1), ROWS, members), jnp.float32),
            pltpu.VMEM((max(len(finished), 1), ROWS, members), jnp.bfloat16),
            pltpu.SemaphoreType.DMA((max(len(finished), 1),)),
        ],
        compiler_params=pltpu.CompilerParams(vmem_limit_bytes=32 * 2**20),
        cost_estimate=pl.CostEstimate(
            flops=2 * products * ROWS * ROWS * members * (parts + 2),
            bytes_accessed=2 * ROWS * members * (len(plan) + 3 * len(finished)),
            transcendentals=0,
        ),
    )(*operands)
    if finished:
        result, outputs = outputs[0], outputs[1:]
    state = {pair: value for pair, value in state.items() if pair not in touched}
    state.update(zip(acc_out, outputs))
    for pair in finished:
        state.pop(pair, None)
    return result, state


def chunk_bounds(pairs):
    first, last = NEAR, pairs - NEAR
    tail = [2, 2]
    bulk = last - first - sum(tail)
    sizes = [(bulk + 1) // 2, bulk // 2] + tail
    bounds = [first]
    for size in sizes:
        if size:
            bounds.append(bounds[-1] + size)
    return list(zip(bounds, bounds[1:]))


def per_device(anomalies, taper):
    rows, members = anomalies.shape
    pairs = rows // ROWS
    ring = lax.axis_size("region")
    down = [(i, i + 1) for i in range(ring - 1)]
    up = [(i + 1, i) for i in range(ring - 1)]
    chunks = chunk_bounds(pairs)

    def cut(first, last):
        return lax.slice_in_dim(anomalies, first * ROWS, last * ROWS, axis=0)

    top, bottom = cut(0, NEAR), cut(pairs - NEAR, pairs)
    tops = shifted(top, "member")
    bottoms = shifted(bottom, "member")
    middles = []
    for first, last in chunks:
        middles.append(shifted(cut(first, last), "member"))

    sets = [([(anomalies, 0, pairs)], top, bottom)]
    for s in range(len(tops)):
        listed = [(tops[s], 0, NEAR)]
        for (first, last), middle in zip(chunks, middles):
            listed.append((middle[s], first, last - first))
        listed.append((bottoms[s], pairs - NEAR, NEAR))
        sets.append((listed, tops[s], bottoms[s]))
    held = []
    for listed, head, tail in sets:
        before = (lax.ppermute(tail, "region", down), -NEAR, NEAR)
        after = (lax.ppermute(head, "region", up), pairs, NEAR)
        held.append([before, after] + listed)
    for turn in range(lax.axis_size("tile") - 1):
        held += [
            [(shifted(array, "tile")[turn], first, count) for array, first, count in listed]
            for listed in list(held)
        ]
    pieces = [
        {first + n: (array, n) for array, first, count in listed for n in range(count)}
        for listed in held
    ]

    owned = set(range(pairs))
    state, result = {}, None

    def steps_for(fresh, before):
        there, steps = set(before), []
        for j in fresh:
            there.add(j)
            near = [i for i in range(j - NEAR, j + NEAR + 1) if i in there and (i in owned or j in owned)]
            while near:
                run = [near[0]]
                while run[-1] + 1 in near:
                    run.append(run[-1] + 1)
                steps.append((j, run[0], len(run)))
                near = near[len(run) :]
        return steps, there

    low = list(range(-NEAR, NEAR))
    high = list(range(pairs - NEAR, pairs + NEAR))
    there, done = set(), set()
    batches = [high, low + list(range(*chunks[0]))] + [list(range(*c)) for c in chunks[1:]]
    for fresh in batches:
        steps, there = steps_for(fresh, there)
        ready = [
            i for i in range(pairs)
            if i not in done and all(k in there for k in range(i - NEAR, i + NEAR + 1))
        ]
        done |= set(ready)
        result, state = run_steps(taper, pieces, steps, owned, state, ready, result, rows, members)
    return result


def solution(mesh):
    in_specs = (P(("groups", "region"), ("member", "tile")), P(("groups", "region"), None))
    out_specs = P(("groups", "region"), ("member", "tile"))

    return jax.shard_map(
        per_device, mesh=mesh, in_specs=in_specs, out_specs=out_specs, check_vma=False
    )
```

```python
import functools

import jax
import jax.numpy as jnp
from jax import lax
from jax.experimental import pallas as pl
from jax.experimental.pallas import tpu as pltpu
from jax.sharding import PartitionSpec as P


MEMBERS = 1024
BLOCK = 128
REACH = 4
SLOTS = 9
FACTOR = 1.0 / (MEMBERS - 1)
PAIR = 2
ROWS = PAIR * BLOCK
NEAR = REACH // PAIR
VMEM_LIMIT = 24 * 2**20


def shifted(value, axis):
    count = lax.axis_size(axis)
    return [
        lax.ppermute(value, axis, [(i, (i + s) % count) for i in range(count)])
        for s in range(1, count)
    ]


def tile_rows(start, count=1):
    return pl.ds(start * ROWS, count * ROWS)


def update_kernel(job, *refs):
    parts = job["parts"]
    plan, steps, owned = job["plan"], job["steps"], job["owned"]
    acc_in, acc_out, finished = job["acc_in"], job["acc_out"], job["finished"]
    writes = job["writes"]
    arrays = job["arrays"]
    taper = refs[0]
    sources = refs[1 : 1 + arrays]
    inputs = dict(zip(acc_in, refs[1 + arrays : 1 + arrays + len(acc_in)]))
    earlier = refs[1 + arrays + len(acc_in) : job["operands"]]
    outs = refs[job["operands"] :]
    if writes:
        out, acc, obuf, out_sem = outs[0], *outs[-3:]
        sent = [
            pltpu.make_async_copy(
                earlier[array].at[n], out.at[tile_rows(pair)], out_sem.at[len(finished) + k]
            )
            for k, (array, n, pair) in enumerate(writes)
        ]
        for copy in sent:
            copy.start()
    else:
        outs, acc = outs[:-1], outs[-1]
        if finished:
            obuf, outs = outs[0], outs[1:]
    carried = outs
    sums = {pair: carried[n] for n, pair in enumerate(acc_out)}
    sums |= {pair: acc.at[n] for n, pair in enumerate(finished)}
    begun = set()

    def piece(pair, part):
        array, start = plan[pair, part]
        return sources[array][tile_rows(start), :]

    def held(pair):
        return jnp.concatenate([piece(pair, part) for part in range(parts)], axis=1)

    def own(pair):
        return piece(pair, 0)

    def add(pair, value):
        if pair in begun:
            value = sums[pair][...] + value
        elif pair in acc_in:
            value = inputs[pair][...] + value
        sums[pair][...] = value
        begun.add(pair)

    def weighted(c, i_pair, j_pair, flip):
        rows = []
        for ii in range(PAIR):
            row = []
            for jj in range(PAIR):
                i, j = i_pair * PAIR + ii, j_pair * PAIR + jj
                slot = (i - j if flip else j - i) + REACH
                if 0 <= slot < SLOTS:
                    weight = taper[j if flip else i, slot] * FACTOR
                    tile = c[ii * BLOCK : (ii + 1) * BLOCK, jj * BLOCK : (jj + 1) * BLOCK]
                    row.append((tile * weight).astype(jnp.bfloat16))
                else:
                    row.append(jnp.zeros((BLOCK, BLOCK), jnp.bfloat16))
            rows.append(jnp.concatenate(row, axis=1))
        return jnp.concatenate(rows, axis=0)

    for j, first, count in steps:
        near = list(range(first, first + count))
        gram = lax.dot_general(
            jnp.concatenate([held(i) for i in near], axis=0),
            held(j),
            (((1,), (1,)), ((), ())),
            preferred_element_type=jnp.float32,
        )
        tiles = {i: gram[n * ROWS : (n + 1) * ROWS] for n, i in enumerate(near)}
        mine = [i for i in near if i in owned]
        if mine:
            value = jnp.dot(
                jnp.concatenate([weighted(tiles[i], i, j, False) for i in mine], axis=0),
                own(j),
                preferred_element_type=jnp.float32,
            )
            for n, i in enumerate(mine):
                add(i, value[n * ROWS : (n + 1) * ROWS])
        others = [i for i in near if i != j]
        if j in owned and others:
            value = None
            for i in others:
                term = jnp.dot(
                    weighted(tiles[i], i, j, True).T, own(i), preferred_element_type=jnp.float32
                )
                value = term if value is None else value + term
            add(j, value)

    for n, pair in enumerate(finished):
        update = (sums if pair in begun else inputs)[pair][...]
        obuf[n] = (own(pair).astype(jnp.float32) - 0.5 * update).astype(jnp.bfloat16)
        if writes:
            sent.append(
                pltpu.make_async_copy(obuf.at[n], out.at[tile_rows(pair)], out_sem.at[n])
            )
            sent[-1].start()
    if writes:
        for copy in sent:
            copy.wait()


def stage_kernel(source, target, sem):
    copy = pltpu.make_async_copy(source, target, sem)
    copy.start()
    copy.wait()


def staged(array):
    return pl.pallas_call(
        stage_kernel,
        out_shape=jax.ShapeDtypeStruct(array.shape, array.dtype),
        in_specs=[pl.BlockSpec(memory_space=pl.ANY)],
        out_specs=pl.BlockSpec(memory_space=pltpu.VMEM),
        scratch_shapes=[pltpu.SemaphoreType.DMA],
        compiler_params=pltpu.CompilerParams(vmem_limit_bytes=VMEM_LIMIT),
        cost_estimate=pl.CostEstimate(
            flops=0, bytes_accessed=2 * array.size, transcendentals=0
        ),
    )(array)


def run_steps(taper, pieces, steps, owned, state, finished, stored, rows, members, last):
    parts = len(pieces)
    needed = set()
    for j, first, count in steps:
        needed |= {j} | set(range(first, first + count))
    needed |= set(finished)
    touched = set()
    for j, first, count in steps:
        near = set(range(first, first + count))
        touched |= near & owned
        if j in owned and near - {j}:
            touched.add(j)
    acc_in = [pair for pair in sorted(touched | set(finished)) if pair in state]
    acc_out = sorted(touched - set(finished))
    arrays, plan = [], {}
    for pair in sorted(needed):
        for part in range(parts):
            array, start = pieces[part][pair]
            known = [n for n, other in enumerate(arrays) if other is array]
            if not known:
                arrays.append(array)
                known = [len(arrays) - 1]
            plan[pair, part] = (known[0], start)
    writes = []
    if last:
        for array, (pairs, _) in enumerate(stored):
            writes += [(array, n, pair) for n, pair in enumerate(pairs)]
    operands = [taper] + arrays + [state[pair] for pair in acc_in]
    if last:
        operands += [block for _, block in stored]
    job = dict(
        parts=parts, plan=plan, steps=steps, owned=owned, acc_in=acc_in, acc_out=acc_out,
        finished=finished, arrays=len(arrays), writes=writes, operands=len(operands),
    )
    inside = pl.BlockSpec(memory_space=pltpu.VMEM)
    specs = [pl.BlockSpec(memory_space=pltpu.SMEM)] + [inside] * (len(operands) - 1)
    products = sum(n for _, _, n in steps)
    count = max(len(finished), 1)
    carries = [jax.ShapeDtypeStruct((ROWS, members), jnp.float32)] * len(acc_out)
    block = (len(finished), ROWS, members)
    scratch = [pltpu.VMEM((count, ROWS, members), jnp.float32)]
    if last:
        shapes = [jax.ShapeDtypeStruct((rows, members), jnp.bfloat16)]
        out_specs = [pl.BlockSpec(memory_space=pl.ANY)]
        scratch += [
            pltpu.VMEM(block, jnp.bfloat16),
            pltpu.SemaphoreType.DMA((len(finished) + len(writes),)),
        ]
    else:
        shapes = [jax.ShapeDtypeStruct(block, jnp.bfloat16)] * int(bool(finished)) + carries
        out_specs = [inside] * len(shapes)
    outputs = pl.pallas_call(
        functools.partial(update_kernel, job),
        out_shape=shapes,
        in_specs=specs,
        out_specs=out_specs,
        scratch_shapes=scratch,
        compiler_params=pltpu.CompilerParams(vmem_limit_bytes=VMEM_LIMIT),
        cost_estimate=pl.CostEstimate(
            flops=2 * products * ROWS * ROWS * members * (parts + 2),
            bytes_accessed=2 * ROWS * members * (len(plan) + 3 * len(finished)),
            transcendentals=0,
        ),
    )(*operands)
    if last:
        return outputs[0], state
    if finished:
        stored.append((finished, outputs[0]))
        outputs = outputs[1:]
    state = {pair: value for pair, value in state.items() if pair not in touched}
    state.update(zip(acc_out, outputs))
    for pair in finished:
        state.pop(pair, None)
    return None, state


def chunk_bounds(pairs):
    first, last = NEAR, pairs - NEAR
    bulk = last - first - 6
    sizes = [2, bulk // 2, bulk - bulk // 2, 2, 2]
    bounds = [first]
    for size in sizes:
        bounds.append(bounds[-1] + size)
    return list(zip(bounds, bounds[1:]))


def per_device(anomalies, taper):
    rows, members = anomalies.shape
    pairs = rows // ROWS
    ring = lax.axis_size("region")
    down = [(i, i + 1) for i in range(ring - 1)]
    up = [(i + 1, i) for i in range(ring - 1)]
    chunks = chunk_bounds(pairs)

    def cut(first, last):
        return lax.slice_in_dim(anomalies, first * ROWS, last * ROWS, axis=0)

    top = cut(0, NEAR)
    anomalies, top = lax.optimization_barrier((anomalies, top))
    bottom = cut(pairs - NEAR, pairs)
    tops = shifted(top, "member")
    bottoms = shifted(bottom, "member")
    middles = []
    for first, last in chunks:
        middles.append(shifted(cut(first, last), "member"))

    sets = [([(anomalies, 0, pairs)], top, bottom)]
    for s in range(len(tops)):
        listed = [(tops[s], 0, NEAR)]
        for (first, last), middle in zip(chunks, middles):
            listed.append((middle[s], first, last - first))
        listed.append((bottoms[s], pairs - NEAR, NEAR))
        sets.append((listed, tops[s], bottoms[s]))
    held = []
    for listed, head, tail in sets:
        before = (lax.ppermute(tail, "region", down), -NEAR, NEAR)
        after = (lax.ppermute(head, "region", up), pairs, NEAR)
        held.append([before, after] + listed)
    for turn in range(lax.axis_size("tile") - 1):
        for listed in list(held):
            there = [(shifted(array, "tile")[turn], first, count) for array, first, count in listed]
            held.append(
                [
                    (staged(array) if count == pairs else array, first, count)
                    for array, first, count in there
                ]
            )
    pieces = [
        {first + n: (array, n) for array, first, count in listed for n in range(count)}
        for listed in held
    ]

    owned = set(range(pairs))
    state, stored = {}, []

    def steps_for(fresh, before):
        there, steps = set(before), []
        for j in fresh:
            there.add(j)
            near = [i for i in range(j - NEAR, j + NEAR + 1) if i in there and (i in owned or j in owned)]
            while near:
                run = [near[0]]
                while run[-1] + 1 in near:
                    run.append(run[-1] + 1)
                steps.append((j, run[0], len(run)))
                near = near[len(run) :]
        return steps, there

    there, done = set(), set()
    low, high = list(range(NEAR)), list(range(pairs - NEAR, pairs))
    around = list(range(-NEAR, 0)) + list(range(pairs, pairs + NEAR))
    batches = [low + list(range(*chunks[0])), high + around] + [list(range(*c)) for c in chunks[1:]]
    for n, fresh in enumerate(batches):
        steps, there = steps_for(fresh, there)
        ready = [
            i for i in range(pairs)
            if i not in done and all(k in there for k in range(i - NEAR, i + NEAR + 1))
        ]
        done |= set(ready)
        result, state = run_steps(
            taper, pieces, steps, owned, state, ready, stored, rows, members,
            n == len(batches) - 1,
        )
    return result


def solution(mesh):
    in_specs = (P(("groups", "region"), ("member", "tile")), P(("groups", "region"), None))
    out_specs = P(("groups", "region"), ("member", "tile"))

    return jax.shard_map(
        per_device, mesh=mesh, in_specs=in_specs, out_specs=out_specs, check_vma=False
    )
```

```python
import functools

import jax
import jax.numpy as jnp
from jax import lax
from jax.experimental import pallas as pl
from jax.experimental.pallas import tpu as pltpu
from jax.sharding import PartitionSpec as P


MEMBERS = 1024
BLOCK = 128
REACH = 4
SLOTS = 9
FACTOR = 1.0 / (MEMBERS - 1)
PAIR = 2
ROWS = PAIR * BLOCK
NEAR = REACH // PAIR
VMEM_LIMIT = 24 * 2**20


def shifted(value, axis):
    count = lax.axis_size(axis)
    return [
        lax.ppermute(value, axis, [(i, (i + s) % count) for i in range(count)])
        for s in range(1, count)
    ]


def tile_rows(start, count=1):
    return pl.ds(start * ROWS, count * ROWS)


def update_kernel(job, *refs):
    parts = job["parts"]
    plan, steps, owned = job["plan"], job["steps"], job["owned"]
    acc_in, acc_out, finished = job["acc_in"], job["acc_out"], job["finished"]
    writes = job["writes"]
    arrays = job["arrays"]
    taper = refs[0]
    sources = refs[1 : 1 + arrays]
    inputs = dict(zip(acc_in, refs[1 + arrays : 1 + arrays + len(acc_in)]))
    earlier = refs[1 + arrays + len(acc_in) : job["operands"]]
    outs = refs[job["operands"] :]
    if writes:
        out, acc, obuf, out_sem = outs[0], *outs[-3:]
        sent = [
            pltpu.make_async_copy(
                earlier[array].at[n], out.at[tile_rows(pair)], out_sem.at[len(finished) + k]
            )
            for k, (array, n, pair) in enumerate(writes)
        ]
        for copy in sent:
            copy.start()
    else:
        outs, acc = outs[:-1], outs[-1]
        if finished:
            obuf, outs = outs[0], outs[1:]
    carried = outs
    sums = {pair: carried[n] for n, pair in enumerate(acc_out)}
    sums |= {pair: acc.at[n] for n, pair in enumerate(finished)}
    begun = set()

    def piece(pair, part):
        array, start = plan[pair, part]
        return sources[array][tile_rows(start), :]

    def held(pair):
        return jnp.concatenate([piece(pair, part) for part in range(parts)], axis=1)

    def own(pair):
        return piece(pair, 0)

    def add(pair, value):
        if pair in begun:
            value = sums[pair][...] + value
        elif pair in acc_in:
            value = inputs[pair][...] + value
        sums[pair][...] = value
        begun.add(pair)

    def weighted(c, i_pair, j_pair, flip):
        rows = []
        for ii in range(PAIR):
            row = []
            for jj in range(PAIR):
                i, j = i_pair * PAIR + ii, j_pair * PAIR + jj
                slot = (i - j if flip else j - i) + REACH
                if 0 <= slot < SLOTS:
                    weight = taper[j if flip else i, slot] * FACTOR
                    tile = c[ii * BLOCK : (ii + 1) * BLOCK, jj * BLOCK : (jj + 1) * BLOCK]
                    row.append((tile * weight).astype(jnp.bfloat16))
                else:
                    row.append(jnp.zeros((BLOCK, BLOCK), jnp.bfloat16))
            rows.append(jnp.concatenate(row, axis=1))
        return jnp.concatenate(rows, axis=0)

    for j, first, count in steps:
        near = list(range(first, first + count))
        gram = lax.dot_general(
            jnp.concatenate([held(i) for i in near], axis=0),
            held(j),
            (((1,), (1,)), ((), ())),
            preferred_element_type=jnp.float32,
        )
        tiles = {i: gram[n * ROWS : (n + 1) * ROWS] for n, i in enumerate(near)}
        mine = [i for i in near if i in owned]
        if mine:
            value = jnp.dot(
                jnp.concatenate([weighted(tiles[i], i, j, False) for i in mine], axis=0),
                own(j),
                preferred_element_type=jnp.float32,
            )
            for n, i in enumerate(mine):
                add(i, value[n * ROWS : (n + 1) * ROWS])
        others = [i for i in near if i != j]
        if j in owned and others:
            value = None
            for i in others:
                term = jnp.dot(
                    weighted(tiles[i], i, j, True).T, own(i), preferred_element_type=jnp.float32
                )
                value = term if value is None else value + term
            add(j, value)

    for n, pair in enumerate(finished):
        update = (sums if pair in begun else inputs)[pair][...]
        obuf[n] = (own(pair).astype(jnp.float32) - 0.5 * update).astype(jnp.bfloat16)
        if writes:
            sent.append(
                pltpu.make_async_copy(obuf.at[n], out.at[tile_rows(pair)], out_sem.at[n])
            )
            sent[-1].start()
    if writes:
        for copy in sent:
            copy.wait()


def stage_kernel(source, target, sem):
    copy = pltpu.make_async_copy(source, target, sem)
    copy.start()
    copy.wait()


def cut_kernel(starts, source, *refs):
    targets, sems = refs[:-1], refs[-1]
    copies = [
        pltpu.make_async_copy(source.at[pl.ds(start, target.shape[0])], target, sems.at[n])
        for n, (start, target) in enumerate(zip(starts, targets))
    ]
    for copy in copies:
        copy.start()
    for copy in copies:
        copy.wait()


def cut_rows(array, ranges):
    shapes = [
        jax.ShapeDtypeStruct(((last - first) * ROWS, array.shape[1]), array.dtype)
        for first, last in ranges
    ]
    return pl.pallas_call(
        functools.partial(cut_kernel, tuple(first * ROWS for first, _ in ranges)),
        out_shape=shapes,
        in_specs=[pl.BlockSpec(memory_space=pl.ANY)],
        out_specs=[pl.BlockSpec(memory_space=pltpu.VMEM)] * len(shapes),
        scratch_shapes=[pltpu.SemaphoreType.DMA((len(shapes),))],
        compiler_params=pltpu.CompilerParams(vmem_limit_bytes=VMEM_LIMIT),
        cost_estimate=pl.CostEstimate(
            flops=0, bytes_accessed=sum(4 * shape.size for shape in shapes), transcendentals=0
        ),
    )(array)


def staged(array):
    return pl.pallas_call(
        stage_kernel,
        out_shape=jax.ShapeDtypeStruct(array.shape, array.dtype),
        in_specs=[pl.BlockSpec(memory_space=pl.ANY)],
        out_specs=pl.BlockSpec(memory_space=pltpu.VMEM),
        scratch_shapes=[pltpu.SemaphoreType.DMA],
        compiler_params=pltpu.CompilerParams(vmem_limit_bytes=VMEM_LIMIT),
        cost_estimate=pl.CostEstimate(
            flops=0, bytes_accessed=2 * array.size, transcendentals=0
        ),
    )(array)


def run_steps(taper, pieces, steps, owned, state, finished, stored, rows, members, last):
    parts = len(pieces)
    needed = set()
    for j, first, count in steps:
        needed |= {j} | set(range(first, first + count))
    needed |= set(finished)
    touched = set()
    for j, first, count in steps:
        near = set(range(first, first + count))
        touched |= near & owned
        if j in owned and near - {j}:
            touched.add(j)
    acc_in = [pair for pair in sorted(touched | set(finished)) if pair in state]
    acc_out = sorted(touched - set(finished))
    arrays, plan = [], {}
    for pair in sorted(needed):
        for part in range(parts):
            array, start = pieces[part][pair]
            known = [n for n, other in enumerate(arrays) if other is array]
            if not known:
                arrays.append(array)
                known = [len(arrays) - 1]
            plan[pair, part] = (known[0], start)
    writes = []
    if last:
        for array, (pairs, _) in enumerate(stored):
            writes += [(array, n, pair) for n, pair in enumerate(pairs)]
    operands = [taper] + arrays + [state[pair] for pair in acc_in]
    if last:
        operands += [block for _, block in stored]
    job = dict(
        parts=parts, plan=plan, steps=steps, owned=owned, acc_in=acc_in, acc_out=acc_out,
        finished=finished, arrays=len(arrays), writes=writes, operands=len(operands),
    )
    inside = pl.BlockSpec(memory_space=pltpu.VMEM)
    specs = [pl.BlockSpec(memory_space=pltpu.SMEM)] + [inside] * (len(operands) - 1)
    products = sum(n for _, _, n in steps)
    count = max(len(finished), 1)
    carries = [jax.ShapeDtypeStruct((ROWS, members), jnp.float32)] * len(acc_out)
    block = (len(finished), ROWS, members)
    scratch = [pltpu.VMEM((count, ROWS, members), jnp.float32)]
    if last:
        shapes = [jax.ShapeDtypeStruct((rows, members), jnp.bfloat16)]
        out_specs = [pl.BlockSpec(memory_space=pl.ANY)]
        scratch += [
            pltpu.VMEM(block, jnp.bfloat16),
            pltpu.SemaphoreType.DMA((len(finished) + len(writes),)),
        ]
    else:
        shapes = [jax.ShapeDtypeStruct(block, jnp.bfloat16)] * int(bool(finished)) + carries
        out_specs = [inside] * len(shapes)
    outputs = pl.pallas_call(
        functools.partial(update_kernel, job),
        out_shape=shapes,
        in_specs=specs,
        out_specs=out_specs,
        scratch_shapes=scratch,
        compiler_params=pltpu.CompilerParams(vmem_limit_bytes=VMEM_LIMIT),
        cost_estimate=pl.CostEstimate(
            flops=2 * products * ROWS * ROWS * members * (parts + 2),
            bytes_accessed=2 * ROWS * members * (len(plan) + 3 * len(finished)),
            transcendentals=0,
        ),
    )(*operands)
    if last:
        return outputs[0], state
    if finished:
        stored.append((finished, outputs[0]))
        outputs = outputs[1:]
    state = {pair: value for pair, value in state.items() if pair not in touched}
    state.update(zip(acc_out, outputs))
    for pair in finished:
        state.pop(pair, None)
    return None, state


def chunk_bounds(pairs):
    first, last = NEAR, pairs - NEAR
    bulk = last - first - 6
    sizes = [2, bulk // 2, bulk - bulk // 2, 2, 2]
    bounds = [first]
    for size in sizes:
        bounds.append(bounds[-1] + size)
    return list(zip(bounds, bounds[1:]))


def per_device(anomalies, taper):
    rows, members = anomalies.shape
    pairs = rows // ROWS
    ring = lax.axis_size("region")
    down = [(i, i + 1) for i in range(ring - 1)]
    up = [(i + 1, i) for i in range(ring - 1)]
    chunks = chunk_bounds(pairs)

    top, bottom, start = cut_rows(anomalies, [(0, NEAR), (pairs - NEAR, pairs), chunks[0]])
    *cuts, inside = cut_rows(anomalies, chunks[1:] + [(0, pairs)])
    cuts = [start] + cuts
    tops = shifted(top, "member")
    bottoms = shifted(bottom, "member")
    middles = []
    for piece in cuts:
        middles.append(shifted(piece, "member"))

    sets = [([(anomalies, 0, pairs)], top, bottom)]
    for s in range(len(tops)):
        listed = [(tops[s], 0, NEAR)]
        for (first, last), middle in zip(chunks, middles):
            listed.append((middle[s], first, last - first))
        listed.append((bottoms[s], pairs - NEAR, NEAR))
        sets.append((listed, tops[s], bottoms[s]))
    held = []
    for listed, head, tail in sets:
        before = (lax.ppermute(tail, "region", down), -NEAR, NEAR)
        after = (lax.ppermute(head, "region", up), pairs, NEAR)
        held.append([before, after] + listed)
    for turn in range(lax.axis_size("tile") - 1):
        for listed in list(held):
            there = [(shifted(array, "tile")[turn], first, count) for array, first, count in listed]
            held.append(
                [
                    (staged(array) if count == pairs else array, first, count)
                    for array, first, count in there
                ]
            )
    held[0] = [(inside if array is anomalies else array, *run) for array, *run in held[0]]
    pieces = [
        {first + n: (array, n) for array, first, count in listed for n in range(count)}
        for listed in held
    ]

    owned = set(range(pairs))
    state, stored = {}, []

    def steps_for(fresh, before):
        there, steps = set(before), []
        for j in fresh:
            there.add(j)
            near = [i for i in range(j - NEAR, j + NEAR + 1) if i in there and (i in owned or j in owned)]
            while near:
                run = [near[0]]
                while run[-1] + 1 in near:
                    run.append(run[-1] + 1)
                steps.append((j, run[0], len(run)))
                near = near[len(run) :]
        return steps, there

    there, done = set(), set()
    low, high = list(range(NEAR)), list(range(pairs - NEAR, pairs))
    around = list(range(-NEAR, 0)) + list(range(pairs, pairs + NEAR))
    batches = [low + list(range(*chunks[0])), high + around] + [list(range(*c)) for c in chunks[1:]]
    for n, fresh in enumerate(batches):
        steps, there = steps_for(fresh, there)
        ready = [
            i for i in range(pairs)
            if i not in done and all(k in there for k in range(i - NEAR, i + NEAR + 1))
        ]
        done |= set(ready)
        result, state = run_steps(
            taper, pieces, steps, owned, state, ready, stored, rows, members,
            n == len(batches) - 1,
        )
    return result


def solution(mesh):
    in_specs = (P(("groups", "region"), ("member", "tile")), P(("groups", "region"), None))
    out_specs = P(("groups", "region"), ("member", "tile"))

    return jax.shard_map(
        per_device, mesh=mesh, in_specs=in_specs, out_specs=out_specs, check_vma=False
    )
```

```python
import functools

import jax
import jax.numpy as jnp
from jax import lax
from jax.experimental import pallas as pl
from jax.experimental.pallas import tpu as pltpu
from jax.sharding import PartitionSpec as P


MEMBERS = 1024
BLOCK = 128
REACH = 4
SLOTS = 9
FACTOR = 1.0 / (MEMBERS - 1)
PAIR = 2
ROWS = PAIR * BLOCK
NEAR = REACH // PAIR
VMEM_LIMIT = 24 * 2**20


def shifted(value, axis):
    count = lax.axis_size(axis)
    return [
        lax.ppermute(value, axis, [(i, (i + s) % count) for i in range(count)])
        for s in range(1, count)
    ]


def tile_rows(start, count=1):
    return pl.ds(start * ROWS, count * ROWS)


def update_kernel(job, *refs):
    parts = job["parts"]
    plan, steps, owned = job["plan"], job["steps"], job["owned"]
    acc_in, acc_out, finished = job["acc_in"], job["acc_out"], job["finished"]
    writes = job["writes"]
    arrays = job["arrays"]
    taper = refs[0]
    sources = refs[1 : 1 + arrays]
    inputs = dict(zip(acc_in, refs[1 + arrays : 1 + arrays + len(acc_in)]))
    earlier = refs[1 + arrays + len(acc_in) : job["operands"]]
    outs = refs[job["operands"] :]
    if job["last"]:
        out, acc, obuf, out_sem = outs[0], *outs[-3:]
        sent = [
            pltpu.make_async_copy(
                earlier[array].at[n], out.at[tile_rows(pair)], out_sem.at[len(finished) + k]
            )
            for k, (array, n, pair) in enumerate(writes)
        ]
        for copy in sent:
            copy.start()
    else:
        outs, acc = outs[:-1], outs[-1]
        if finished:
            obuf, outs = outs[0], outs[1:]
    carried = outs
    sums = {pair: carried[n] for n, pair in enumerate(acc_out)}
    sums |= {pair: acc.at[n] for n, pair in enumerate(finished)}
    begun = set()

    def piece(pair, part):
        array, start = plan[pair, part]
        return sources[array][tile_rows(start), :]

    def held(pair):
        return jnp.concatenate([piece(pair, part) for part in range(parts)], axis=1)

    def own(pair):
        return piece(pair, 0)

    def add(pair, value):
        if pair in begun:
            value = sums[pair][...] + value
        elif pair in acc_in:
            value = inputs[pair][...] + value
        sums[pair][...] = value
        begun.add(pair)

    def weighted(c, i_pair, j_pair, flip):
        rows = []
        for ii in range(PAIR):
            row = []
            for jj in range(PAIR):
                i, j = i_pair * PAIR + ii, j_pair * PAIR + jj
                slot = (i - j if flip else j - i) + REACH
                if 0 <= slot < SLOTS:
                    weight = taper[slot, j if flip else i] * FACTOR
                    tile = c[ii * BLOCK : (ii + 1) * BLOCK, jj * BLOCK : (jj + 1) * BLOCK]
                    row.append((tile * weight).astype(jnp.bfloat16))
                else:
                    row.append(jnp.zeros((BLOCK, BLOCK), jnp.bfloat16))
            rows.append(jnp.concatenate(row, axis=1))
        return jnp.concatenate(rows, axis=0)

    for j, first, count in steps:
        near = list(range(first, first + count))
        left = jnp.concatenate([held(i) for i in near], axis=0)
        half = count * ROWS // 2
        gram = jnp.concatenate(
            [
                lax.dot_general(
                    part,
                    held(j),
                    (((1,), (1,)), ((), ())),
                    preferred_element_type=jnp.float32,
                )
                for part in (left[:half], left[half:])
            ],
            axis=0,
        )
        tiles = {i: gram[n * ROWS : (n + 1) * ROWS] for n, i in enumerate(near)}
        mine = [i for i in near if i in owned]
        if mine:
            value = jnp.dot(
                jnp.concatenate([weighted(tiles[i], i, j, False) for i in mine], axis=0),
                own(j),
                preferred_element_type=jnp.float32,
            )
            for n, i in enumerate(mine):
                add(i, value[n * ROWS : (n + 1) * ROWS])
        others = [i for i in near if i != j]
        if j in owned and others:
            value = None
            for i in others:
                term = jnp.dot(
                    weighted(tiles[i], i, j, True).T, own(i), preferred_element_type=jnp.float32
                )
                value = term if value is None else value + term
            add(j, value)

    for n, pair in enumerate(finished):
        update = (sums if pair in begun else inputs)[pair][...]
        obuf[n] = (own(pair).astype(jnp.float32) - 0.5 * update).astype(jnp.bfloat16)
        if job["last"]:
            sent.append(
                pltpu.make_async_copy(obuf.at[n], out.at[tile_rows(pair)], out_sem.at[n])
            )
            sent[-1].start()
    if job["last"]:
        for copy in sent:
            copy.wait()


def stage_kernel(source, target, sem):
    copy = pltpu.make_async_copy(source, target, sem)
    copy.start()
    copy.wait()


def cut_kernel(starts, source, *refs):
    targets, sems = refs[:-1], refs[-1]
    copies = [
        pltpu.make_async_copy(source.at[pl.ds(start, target.shape[0])], target, sems.at[n])
        for n, (start, target) in enumerate(zip(starts, targets))
    ]
    for copy in copies:
        copy.start()
    for copy in copies:
        copy.wait()


def cut_rows(array, ranges, limit=VMEM_LIMIT):
    shapes = [
        jax.ShapeDtypeStruct(((last - first) * ROWS, array.shape[1]), array.dtype)
        for first, last in ranges
    ]
    return pl.pallas_call(
        functools.partial(cut_kernel, tuple(first * ROWS for first, _ in ranges)),
        out_shape=shapes,
        in_specs=[pl.BlockSpec(memory_space=pltpu.HBM)],
        out_specs=[pl.BlockSpec(memory_space=pltpu.VMEM)] * len(shapes),
        scratch_shapes=[pltpu.SemaphoreType.DMA((len(shapes),))],
        compiler_params=pltpu.CompilerParams(vmem_limit_bytes=limit),
        cost_estimate=pl.CostEstimate(
            flops=0, bytes_accessed=sum(4 * shape.size for shape in shapes), transcendentals=0
        ),
    )(array)


def staged(array):
    return pl.pallas_call(
        stage_kernel,
        out_shape=jax.ShapeDtypeStruct(array.shape, array.dtype),
        in_specs=[pl.BlockSpec(memory_space=pl.ANY)],
        out_specs=pl.BlockSpec(memory_space=pltpu.VMEM),
        scratch_shapes=[pltpu.SemaphoreType.DMA],
        compiler_params=pltpu.CompilerParams(vmem_limit_bytes=VMEM_LIMIT),
        cost_estimate=pl.CostEstimate(
            flops=0, bytes_accessed=2 * array.size, transcendentals=0
        ),
    )(array)


def join_kernel(*refs):
    sources, target, sems = refs[:-2], refs[-2], refs[-1]
    copies, at = [], 0
    for n, source in enumerate(sources):
        copies.append(
            pltpu.make_async_copy(source, target.at[pl.ds(at, source.shape[0])], sems.at[n])
        )
        at += source.shape[0]
    for copy in copies:
        copy.start()
    for copy in copies:
        copy.wait()


def joined(arrays):
    rows = sum(array.shape[0] for array in arrays)
    return pl.pallas_call(
        join_kernel,
        out_shape=jax.ShapeDtypeStruct((rows, arrays[0].shape[1]), arrays[0].dtype),
        in_specs=[pl.BlockSpec(memory_space=pl.ANY)] * len(arrays),
        out_specs=pl.BlockSpec(memory_space=pltpu.VMEM),
        scratch_shapes=[pltpu.SemaphoreType.DMA((len(arrays),))],
        compiler_params=pltpu.CompilerParams(vmem_limit_bytes=VMEM_LIMIT),
        cost_estimate=pl.CostEstimate(
            flops=0, bytes_accessed=4 * rows * arrays[0].shape[1], transcendentals=0
        ),
    )(*arrays)


def run_steps(taper, pieces, steps, owned, state, finished, stored, rows, members, last):
    parts = len(pieces)
    needed = set()
    for j, first, count in steps:
        needed |= {j} | set(range(first, first + count))
    needed |= set(finished)
    touched = set()
    for j, first, count in steps:
        near = set(range(first, first + count))
        touched |= near & owned
        if j in owned and near - {j}:
            touched.add(j)
    acc_in = [pair for pair in sorted(touched | set(finished)) if pair in state]
    acc_out = sorted(touched - set(finished))
    arrays, plan = [], {}
    for pair in sorted(needed):
        for part in range(parts):
            array, start = pieces[part][pair]
            known = [n for n, other in enumerate(arrays) if other is array]
            if not known:
                arrays.append(array)
                known = [len(arrays) - 1]
            plan[pair, part] = (known[0], start)
    writes = []
    if last:
        for array, (pairs, _) in enumerate(stored):
            writes += [(array, n, pair) for n, pair in enumerate(pairs)]
    operands = [taper.T] + arrays + [state[pair] for pair in acc_in]
    if last:
        operands += [block for _, block in stored]
    job = dict(
        parts=parts, plan=plan, steps=steps, owned=owned, acc_in=acc_in, acc_out=acc_out,
        finished=finished, arrays=len(arrays), writes=writes, operands=len(operands),
        last=last,
    )
    inside = pl.BlockSpec(memory_space=pltpu.VMEM)
    specs = [pl.BlockSpec(memory_space=pltpu.SMEM)] + [inside] * (len(operands) - 1)
    products = sum(n for _, _, n in steps)
    count = max(len(finished), 1)
    carries = [jax.ShapeDtypeStruct((ROWS, members), jnp.float32)] * len(acc_out)
    block = (len(finished), ROWS, members)
    scratch = [pltpu.VMEM((count, ROWS, members), jnp.float32)]
    if last:
        shapes = [jax.ShapeDtypeStruct((rows, members), jnp.bfloat16)]
        out_specs = [pl.BlockSpec(memory_space=pl.ANY)]
        scratch += [
            pltpu.VMEM(block, jnp.bfloat16),
            pltpu.SemaphoreType.DMA((len(finished) + len(writes),)),
        ]
    else:
        shapes = [jax.ShapeDtypeStruct(block, jnp.bfloat16)] * int(bool(finished)) + carries
        out_specs = [inside] * len(shapes)
    outputs = pl.pallas_call(
        functools.partial(update_kernel, job),
        out_shape=shapes,
        in_specs=specs,
        out_specs=out_specs,
        scratch_shapes=scratch,
        compiler_params=pltpu.CompilerParams(vmem_limit_bytes=VMEM_LIMIT),
        cost_estimate=pl.CostEstimate(
            flops=2 * products * ROWS * ROWS * members * (parts + 2),
            bytes_accessed=2 * ROWS * members * (len(plan) + 3 * len(finished)),
            transcendentals=0,
        ),
    )(*operands)
    if last:
        return outputs[0], state
    if finished:
        stored.append((finished, outputs[0]))
        outputs = outputs[1:]
    state = {pair: value for pair, value in state.items() if pair not in touched}
    state.update(zip(acc_out, outputs))
    for pair in finished:
        state.pop(pair, None)
    return None, state


def chunk_bounds(pairs):
    first, last = NEAR, pairs - NEAR
    bulk = last - first - 6
    sizes = [2, bulk // 2, bulk - bulk // 2, 2, 2]
    bounds = [first]
    for size in sizes:
        bounds.append(bounds[-1] + size)
    return list(zip(bounds, bounds[1:]))


def per_device(anomalies, taper):
    rows, members = anomalies.shape
    pairs = rows // ROWS
    ring = lax.axis_size("region")
    down = [(i, i + 1) for i in range(ring - 1)]
    up = [(i + 1, i) for i in range(ring - 1)]
    chunks = chunk_bounds(pairs)

    top, bottom, start = cut_rows(
        anomalies, [(0, NEAR), (pairs - NEAR, pairs), chunks[0]], 60 * 2**20
    )
    *cuts, inside = cut_rows(anomalies, chunks[1:] + [(0, pairs)])
    cuts = [start] + cuts
    tops = shifted(top, "member")
    bottoms = shifted(bottom, "member")
    middles = []
    for piece in cuts:
        middles.append(shifted(piece, "member"))

    heads, tails = joined([top] + tops), joined([bottom] + bottoms)
    before = lax.ppermute(tails, "region", down)
    after = lax.ppermute(heads, "region", up)

    def run(array, first, count, start=0):
        return {first + n: (array, start + n) for n in range(count)}

    held = [run(inside, 0, pairs)]
    for s in range(len(tops)):
        listed = run(tops[s], 0, NEAR) | run(bottoms[s], pairs - NEAR, NEAR)
        for (first, last), middle in zip(chunks, middles):
            listed |= run(middle[s], first, last - first)
        held.append(listed)
    for n, listed in enumerate(held):
        listed |= run(before, -NEAR, NEAR, n * NEAR) | run(after, pairs, NEAR, n * NEAR)

    pieces = list(held)
    for turn in range(lax.axis_size("tile") - 1):
        sent = {}

        def passed(array):
            if id(array) not in sent:
                if array is inside:
                    moved = shifted(anomalies, "tile")[turn]
                    sent[id(array)] = staged(moved)
                else:
                    sent[id(array)] = shifted(array, "tile")[turn]
            return sent[id(array)]

        for listed in held:
            pieces.append({pair: (passed(array), n) for pair, (array, n) in listed.items()})

    owned = set(range(pairs))
    state, stored = {}, []

    def steps_for(fresh, before):
        there, steps = set(before), []
        for j in fresh:
            there.add(j)
            near = [i for i in range(j - NEAR, j + NEAR + 1) if i in there and (i in owned or j in owned)]
            while near:
                run = [near[0]]
                while run[-1] + 1 in near:
                    run.append(run[-1] + 1)
                steps.append((j, run[0], len(run)))
                near = near[len(run) :]
        return steps, there

    there, done = set(), set()
    low, high = list(range(NEAR)), list(range(pairs - NEAR, pairs))
    around = list(range(-NEAR, 0)) + list(range(pairs, pairs + NEAR))
    batches = [low + list(range(*chunks[0])), list(range(*chunks[1])), high + around]
    batches += [list(range(*c)) for c in chunks[2:]]
    for n, fresh in enumerate(batches):
        steps, there = steps_for(fresh, there)
        ready = [
            i for i in range(pairs)
            if i not in done and all(k in there for k in range(i - NEAR, i + NEAR + 1))
        ]
        done |= set(ready)
        result, state = run_steps(
            taper, pieces, steps, owned, state, ready, stored, rows, members,
            n == len(batches) - 1,
        )
    return result


def solution(mesh):
    in_specs = (P(("groups", "region"), ("member", "tile")), P(("groups", "region"), None))
    out_specs = P(("groups", "region"), ("member", "tile"))

    return jax.shard_map(
        per_device, mesh=mesh, in_specs=in_specs, out_specs=out_specs, check_vma=False
    )
```

```python
import functools

import jax
import jax.numpy as jnp
from jax import lax
from jax.experimental import pallas as pl
from jax.experimental.pallas import tpu as pltpu
from jax.sharding import PartitionSpec as P


MEMBERS = 1024
BLOCK = 128
REACH = 4
SLOTS = 9
FACTOR = 1.0 / (MEMBERS - 1)
PAIR = 2
ROWS = PAIR * BLOCK
NEAR = REACH // PAIR
VMEM_LIMIT = 24 * 2**20


def shifted(value, axis):
    count = lax.axis_size(axis)
    return [
        lax.ppermute(value, axis, [(i, (i + s) % count) for i in range(count)])
        for s in range(1, count)
    ]


def tile_rows(start, count=1):
    return pl.ds(start * ROWS, count * ROWS)


def update_kernel(job, *refs):
    parts = job["parts"]
    plan, steps, owned = job["plan"], job["steps"], job["owned"]
    acc_in, acc_out, finished = job["acc_in"], job["acc_out"], job["finished"]
    writes = job["writes"]
    arrays = job["arrays"]
    taper = refs[0]
    sources = refs[1 : 1 + arrays]
    inputs = dict(zip(acc_in, refs[1 + arrays : 1 + arrays + len(acc_in)]))
    earlier = refs[1 + arrays + len(acc_in) : job["operands"]]
    outs = refs[job["operands"] :]
    if job["last"]:
        out, acc, obuf, out_sem = outs[0], *outs[-3:]
        sent = [
            pltpu.make_async_copy(
                earlier[array].at[n], out.at[tile_rows(pair)], out_sem.at[len(finished) + k]
            )
            for k, (array, n, pair) in enumerate(writes)
        ]
        for copy in sent:
            copy.start()
    else:
        outs, acc = outs[:-1], outs[-1]
        if finished:
            obuf, outs = outs[0], outs[1:]
    carried = outs
    sums = {pair: carried[n] for n, pair in enumerate(acc_out)}
    sums |= {pair: acc.at[n] for n, pair in enumerate(finished)}
    begun = set()

    def piece(pair, part):
        array, start = plan[pair, part]
        return sources[array][tile_rows(start), :]

    def held(pair):
        return jnp.concatenate([piece(pair, part) for part in range(parts)], axis=1)

    def own(pair):
        return piece(pair, 0)

    def add(pair, value):
        if pair in begun:
            value = sums[pair][...] + value
        elif pair in acc_in:
            value = inputs[pair][...] + value
        sums[pair][...] = value
        begun.add(pair)

    def weighted(c, i_pair, j_pair, flip):
        rows = []
        for ii in range(PAIR):
            row = []
            for jj in range(PAIR):
                i, j = i_pair * PAIR + ii, j_pair * PAIR + jj
                slot = (i - j if flip else j - i) + REACH
                if 0 <= slot < SLOTS:
                    weight = taper[slot, j if flip else i] * FACTOR
                    tile = c[ii * BLOCK : (ii + 1) * BLOCK, jj * BLOCK : (jj + 1) * BLOCK]
                    row.append((tile * weight).astype(jnp.bfloat16))
                else:
                    row.append(jnp.zeros((BLOCK, BLOCK), jnp.bfloat16))
            rows.append(jnp.concatenate(row, axis=1))
        return jnp.concatenate(rows, axis=0)

    for j, first, count in steps:
        near = list(range(first, first + count))
        left = jnp.concatenate([held(i) for i in near], axis=0)
        half = count * ROWS // 2
        gram = jnp.concatenate(
            [
                lax.dot_general(
                    part,
                    held(j),
                    (((1,), (1,)), ((), ())),
                    preferred_element_type=jnp.float32,
                )
                for part in (left[:half], left[half:])
            ],
            axis=0,
        )
        tiles = {i: gram[n * ROWS : (n + 1) * ROWS] for n, i in enumerate(near)}
        mine = [i for i in near if i in owned]
        if mine:
            value = jnp.dot(
                jnp.concatenate([weighted(tiles[i], i, j, False) for i in mine], axis=0),
                own(j),
                preferred_element_type=jnp.float32,
            )
            for n, i in enumerate(mine):
                add(i, value[n * ROWS : (n + 1) * ROWS])
        others = [i for i in near if i != j]
        if j in owned and others:
            value = None
            for i in others:
                term = jnp.dot(
                    weighted(tiles[i], i, j, True).T, own(i), preferred_element_type=jnp.float32
                )
                value = term if value is None else value + term
            add(j, value)

    for n, pair in enumerate(finished):
        update = (sums if pair in begun else inputs)[pair][...]
        obuf[n] = (own(pair).astype(jnp.float32) - 0.5 * update).astype(jnp.bfloat16)
        if job["last"]:
            sent.append(
                pltpu.make_async_copy(obuf.at[n], out.at[tile_rows(pair)], out_sem.at[n])
            )
            sent[-1].start()
    if job["last"]:
        for copy in sent:
            copy.wait()


def stage_kernel(source, target, sem):
    copy = pltpu.make_async_copy(source, target, sem)
    copy.start()
    copy.wait()


def cut_kernel(starts, source, *refs):
    targets, sems = refs[:-1], refs[-1]
    copies = [
        pltpu.make_async_copy(source.at[pl.ds(start, target.shape[0])], target, sems.at[n])
        for n, (start, target) in enumerate(zip(starts, targets))
    ]
    for copy in copies:
        copy.start()
    for copy in copies:
        copy.wait()


def cut_rows(array, ranges, limit=VMEM_LIMIT):
    shapes = [
        jax.ShapeDtypeStruct(((last - first) * ROWS, array.shape[1]), array.dtype)
        for first, last in ranges
    ]
    return pl.pallas_call(
        functools.partial(cut_kernel, tuple(first * ROWS for first, _ in ranges)),
        out_shape=shapes,
        in_specs=[pl.BlockSpec(memory_space=pltpu.HBM)],
        out_specs=[pl.BlockSpec(memory_space=pltpu.VMEM)] * len(shapes),
        scratch_shapes=[pltpu.SemaphoreType.DMA((len(shapes),))],
        compiler_params=pltpu.CompilerParams(vmem_limit_bytes=limit),
        cost_estimate=pl.CostEstimate(
            flops=0, bytes_accessed=sum(4 * shape.size for shape in shapes), transcendentals=0
        ),
    )(array)


def staged(array):
    return pl.pallas_call(
        stage_kernel,
        out_shape=jax.ShapeDtypeStruct(array.shape, array.dtype),
        in_specs=[pl.BlockSpec(memory_space=pl.ANY)],
        out_specs=pl.BlockSpec(memory_space=pltpu.VMEM),
        scratch_shapes=[pltpu.SemaphoreType.DMA],
        compiler_params=pltpu.CompilerParams(vmem_limit_bytes=VMEM_LIMIT),
        cost_estimate=pl.CostEstimate(
            flops=0, bytes_accessed=2 * array.size, transcendentals=0
        ),
    )(array)


def join_kernel(*refs):
    sources, target, sems = refs[:-2], refs[-2], refs[-1]
    copies, at = [], 0
    for n, source in enumerate(sources):
        copies.append(
            pltpu.make_async_copy(source, target.at[pl.ds(at, source.shape[0])], sems.at[n])
        )
        at += source.shape[0]
    for copy in copies:
        copy.start()
    for copy in copies:
        copy.wait()


def joined(arrays):
    rows = sum(array.shape[0] for array in arrays)
    return pl.pallas_call(
        join_kernel,
        out_shape=jax.ShapeDtypeStruct((rows, arrays[0].shape[1]), arrays[0].dtype),
        in_specs=[pl.BlockSpec(memory_space=pl.ANY)] * len(arrays),
        out_specs=pl.BlockSpec(memory_space=pltpu.VMEM),
        scratch_shapes=[pltpu.SemaphoreType.DMA((len(arrays),))],
        compiler_params=pltpu.CompilerParams(vmem_limit_bytes=VMEM_LIMIT),
        cost_estimate=pl.CostEstimate(
            flops=0, bytes_accessed=4 * rows * arrays[0].shape[1], transcendentals=0
        ),
    )(*arrays)


def run_steps(taper, pieces, steps, owned, state, finished, stored, rows, members, last):
    parts = len(pieces)
    needed = set()
    for j, first, count in steps:
        needed |= {j} | set(range(first, first + count))
    needed |= set(finished)
    touched = set()
    for j, first, count in steps:
        near = set(range(first, first + count))
        touched |= near & owned
        if j in owned and near - {j}:
            touched.add(j)
    acc_in = [pair for pair in sorted(touched | set(finished)) if pair in state]
    acc_out = sorted(touched - set(finished))
    arrays, plan = [], {}
    for pair in sorted(needed):
        for part in range(parts):
            array, start = pieces[part][pair]
            known = [n for n, other in enumerate(arrays) if other is array]
            if not known:
                arrays.append(array)
                known = [len(arrays) - 1]
            plan[pair, part] = (known[0], start)
    writes = []
    if last:
        for array, (pairs, _) in enumerate(stored):
            writes += [(array, n, pair) for n, pair in enumerate(pairs)]
    operands = [taper.T] + arrays + [state[pair] for pair in acc_in]
    if last:
        operands += [block for _, block in stored]
    job = dict(
        parts=parts, plan=plan, steps=steps, owned=owned, acc_in=acc_in, acc_out=acc_out,
        finished=finished, arrays=len(arrays), writes=writes, operands=len(operands),
        last=last,
    )
    inside = pl.BlockSpec(memory_space=pltpu.VMEM)
    specs = [pl.BlockSpec(memory_space=pltpu.SMEM)] + [inside] * (len(operands) - 1)
    products = sum(n for _, _, n in steps)
    count = max(len(finished), 1)
    carries = [jax.ShapeDtypeStruct((ROWS, members), jnp.float32)] * len(acc_out)
    block = (len(finished), ROWS, members)
    scratch = [pltpu.VMEM((count, ROWS, members), jnp.float32)]
    if last:
        shapes = [jax.ShapeDtypeStruct((rows, members), jnp.bfloat16)]
        out_specs = [pl.BlockSpec(memory_space=pl.ANY)]
        scratch += [
            pltpu.VMEM(block, jnp.bfloat16),
            pltpu.SemaphoreType.DMA((len(finished) + len(writes),)),
        ]
    else:
        shapes = [jax.ShapeDtypeStruct(block, jnp.bfloat16)] * int(bool(finished)) + carries
        out_specs = [inside] * len(shapes)
    outputs = pl.pallas_call(
        functools.partial(update_kernel, job),
        out_shape=shapes,
        in_specs=specs,
        out_specs=out_specs,
        scratch_shapes=scratch,
        compiler_params=pltpu.CompilerParams(vmem_limit_bytes=VMEM_LIMIT),
        cost_estimate=pl.CostEstimate(
            flops=2 * products * ROWS * ROWS * members * (parts + 2),
            bytes_accessed=2 * ROWS * members * (len(plan) + 3 * len(finished)),
            transcendentals=0,
        ),
    )(*operands)
    if last:
        return outputs[0], state
    if finished:
        stored.append((finished, outputs[0]))
        outputs = outputs[1:]
    state = {pair: value for pair, value in state.items() if pair not in touched}
    state.update(zip(acc_out, outputs))
    for pair in finished:
        state.pop(pair, None)
    return None, state


def chunk_bounds(pairs):
    first, last = NEAR, pairs - NEAR
    bulk = last - first - 6
    sizes = [2, bulk // 2, bulk - bulk // 2, 2, 2]
    bounds = [first]
    for size in sizes:
        bounds.append(bounds[-1] + size)
    return list(zip(bounds, bounds[1:]))


def per_device(anomalies, taper):
    rows, members = anomalies.shape
    pairs = rows // ROWS
    ring = lax.axis_size("region")
    down = [(i, i + 1) for i in range(ring - 1)]
    up = [(i + 1, i) for i in range(ring - 1)]
    chunks = chunk_bounds(pairs)

    top, bottom, start = cut_rows(
        anomalies, [(0, NEAR), (pairs - NEAR, pairs), chunks[0]], 24 * 2**20
    )
    *cuts, inside = cut_rows(anomalies, chunks[1:] + [(0, pairs)])
    cuts = [start] + cuts
    tops = shifted(top, "member")
    bottoms = shifted(bottom, "member")
    middles = []
    for piece in cuts:
        middles.append(shifted(piece, "member"))

    heads = joined([top] + tops)
    after = lax.ppermute(heads, "region", up)
    tails = joined([bottom] + bottoms)
    before = lax.ppermute(tails, "region", down)

    def run(array, first, count, start=0):
        return {first + n: (array, start + n) for n in range(count)}

    held = [run(inside, 0, pairs)]
    for s in range(len(tops)):
        listed = run(tops[s], 0, NEAR) | run(bottoms[s], pairs - NEAR, NEAR)
        for (first, last), middle in zip(chunks, middles):
            listed |= run(middle[s], first, last - first)
        held.append(listed)
    for n, listed in enumerate(held):
        listed |= run(before, -NEAR, NEAR, n * NEAR) | run(after, pairs, NEAR, n * NEAR)

    pieces = list(held)
    for turn in range(lax.axis_size("tile") - 1):
        sent = {}

        def passed(array):
            if id(array) not in sent:
                if array is inside:
                    moved = shifted(inside, "tile")[turn]
                    sent[id(array)] = staged(moved)
                else:
                    sent[id(array)] = shifted(array, "tile")[turn]
            return sent[id(array)]

        for listed in held:
            pieces.append({pair: (passed(array), n) for pair, (array, n) in listed.items()})

    owned = set(range(pairs))
    state, stored = {}, []

    def steps_for(fresh, before):
        there, steps = set(before), []
        for j in fresh:
            there.add(j)
            near = [i for i in range(j - NEAR, j + NEAR + 1) if i in there and (i in owned or j in owned)]
            while near:
                run = [near[0]]
                while run[-1] + 1 in near:
                    run.append(run[-1] + 1)
                steps.append((j, run[0], len(run)))
                near = near[len(run) :]
        return steps, there

    there, done = set(), set()
    low, high = list(range(NEAR)), list(range(pairs - NEAR, pairs))
    around = list(range(-NEAR, 0)) + list(range(pairs, pairs + NEAR))
    batches = [low + list(range(*chunks[0])), high + around]
    batches += [list(range(*c)) for c in chunks[1:]]
    for n, fresh in enumerate(batches):
        steps, there = steps_for(fresh, there)
        ready = [
            i for i in range(pairs)
            if i not in done and all(k in there for k in range(i - NEAR, i + NEAR + 1))
        ]
        done |= set(ready)
        result, state = run_steps(
            taper, pieces, steps, owned, state, ready, stored, rows, members,
            n == len(batches) - 1,
        )
    return result


def solution(mesh):
    in_specs = (P(("groups", "region"), ("member", "tile")), P(("groups", "region"), None))
    out_specs = P(("groups", "region"), ("member", "tile"))

    return jax.shard_map(
        per_device, mesh=mesh, in_specs=in_specs, out_specs=out_specs, check_vma=False
    )
```

```python
import functools

import jax
import jax.numpy as jnp
from jax import lax
from jax.experimental import pallas as pl
from jax.experimental.pallas import tpu as pltpu
from jax.sharding import PartitionSpec as P


MEMBERS = 1024
BLOCK = 128
REACH = 4
SLOTS = 9
FACTOR = 1.0 / (MEMBERS - 1)
PAIR = 2
ROWS = PAIR * BLOCK
NEAR = REACH // PAIR
VMEM_LIMIT = 24 * 2**20


def shifted(value, axis):
    count = lax.axis_size(axis)
    return [
        lax.ppermute(value, axis, [(i, (i + s) % count) for i in range(count)])
        for s in range(1, count)
    ]


def tile_rows(start, count=1):
    return pl.ds(start * ROWS, count * ROWS)


def gram_rows(held, j, near, begin=None):
    left = jnp.concatenate([held(i) for i in near], axis=0)
    half = left.shape[0] // 2
    halves = []
    for n in range(2):
        part = lax.dot_general(
            left[n * half : (n + 1) * half],
            held(j),
            (((1,), (1,)), ((), ())),
            preferred_element_type=jnp.float32,
        )
        halves.append(part if begin is None else part + begin[pl.ds(n * half, half), :])
    return jnp.concatenate(halves, axis=0)


def partial_kernel(parts, plan, steps, arrays, *refs):
    sources, begins, outs = refs[:arrays], refs[arrays : -len(steps)], refs[-len(steps) :]

    def held(pair):
        pieces = [plan[pair, part] for part in parts]
        return jnp.concatenate([sources[n][tile_rows(start), :] for n, start in pieces], axis=1)

    for k, (j, first, count) in enumerate(steps):
        near = list(range(first, first + count))
        outs[k][...] = gram_rows(held, j, near, begins[k] if begins else None)


def planned(pieces, parts, pairs):
    arrays, plan = [], {}
    for pair in sorted(pairs):
        for part in parts:
            array, start = pieces[part][pair]
            known = [n for n, other in enumerate(arrays) if other is array]
            if not known:
                arrays.append(array)
                known = [len(arrays) - 1]
            plan[pair, part] = (known[0], start)
    return arrays, plan


def touched_by(steps):
    pairs = set()
    for j, first, count in steps:
        pairs |= {j} | set(range(first, first + count))
    return pairs


def partial_grams(pieces, parts, steps, begins):
    arrays, plan = planned(pieces, parts, touched_by(steps))
    inside = pl.BlockSpec(memory_space=pltpu.VMEM)
    products = sum(n for _, _, n in steps)
    members = arrays[0].shape[1]
    return pl.pallas_call(
        functools.partial(partial_kernel, parts, plan, steps, len(arrays)),
        out_shape=[jax.ShapeDtypeStruct((n * ROWS, ROWS), jnp.float32) for _, _, n in steps],
        in_specs=[inside] * (len(arrays) + len(begins)),
        out_specs=[inside] * len(steps),
        compiler_params=pltpu.CompilerParams(vmem_limit_bytes=VMEM_LIMIT),
        cost_estimate=pl.CostEstimate(
            flops=2 * products * ROWS * ROWS * members * len(parts),
            bytes_accessed=4 * products * ROWS * ROWS,
            transcendentals=0,
        ),
    )(*arrays, *begins)


def update_kernel(job, *refs):
    parts = job["parts"]
    plan, steps, owned = job["plan"], job["steps"], job["owned"]
    acc_in, acc_out, finished = job["acc_in"], job["acc_out"], job["finished"]
    writes = job["writes"]
    arrays = job["arrays"]
    taper = refs[0]
    sources = refs[1 : 1 + arrays]
    inputs = dict(zip(acc_in, refs[1 + arrays : 1 + arrays + len(acc_in)]))
    begins = refs[1 + arrays + len(acc_in) : job["earlier"]]
    earlier = refs[job["earlier"] : job["operands"]]
    outs = refs[job["operands"] :]
    if job["last"]:
        out, acc, obuf, out_sem = outs[0], *outs[-3:]
        sent = [
            pltpu.make_async_copy(
                earlier[array].at[n], out.at[tile_rows(pair)], out_sem.at[len(finished) + k]
            )
            for k, (array, n, pair) in enumerate(writes)
        ]
        for copy in sent:
            copy.start()
    else:
        outs, acc = outs[:-1], outs[-1]
        if finished:
            obuf, outs = outs[0], outs[1:]
    carried = outs
    sums = {pair: carried[n] for n, pair in enumerate(acc_out)}
    sums |= {pair: acc.at[n] for n, pair in enumerate(finished)}
    begun = set()

    def piece(pair, part):
        array, start = plan[pair, part]
        return sources[array][tile_rows(start), :]

    def held(pair):
        return jnp.concatenate([piece(pair, part) for part in parts], axis=1)

    def own(pair):
        return piece(pair, 0)

    def add(pair, value):
        if pair in begun:
            value = sums[pair][...] + value
        elif pair in acc_in:
            value = inputs[pair][...] + value
        sums[pair][...] = value
        begun.add(pair)

    def weighted(c, i_pair, j_pair, flip):
        rows = []
        for ii in range(PAIR):
            row = []
            for jj in range(PAIR):
                i, j = i_pair * PAIR + ii, j_pair * PAIR + jj
                slot = (i - j if flip else j - i) + REACH
                if 0 <= slot < SLOTS:
                    weight = taper[slot, j if flip else i] * FACTOR
                    tile = c[ii * BLOCK : (ii + 1) * BLOCK, jj * BLOCK : (jj + 1) * BLOCK]
                    row.append((tile * weight).astype(jnp.bfloat16))
                else:
                    row.append(jnp.zeros((BLOCK, BLOCK), jnp.bfloat16))
            rows.append(jnp.concatenate(row, axis=1))
        return jnp.concatenate(rows, axis=0)

    for k, (j, first, count) in enumerate(steps):
        near = list(range(first, first + count))
        gram = gram_rows(held, j, near, begins[k] if begins else None)
        tiles = {i: gram[n * ROWS : (n + 1) * ROWS] for n, i in enumerate(near)}
        mine = [i for i in near if i in owned]
        if mine:
            value = jnp.dot(
                jnp.concatenate([weighted(tiles[i], i, j, False) for i in mine], axis=0),
                own(j),
                preferred_element_type=jnp.float32,
            )
            for n, i in enumerate(mine):
                add(i, value[n * ROWS : (n + 1) * ROWS])
        others = [i for i in near if i != j]
        if j in owned and others:
            value = None
            for i in others:
                term = jnp.dot(
                    weighted(tiles[i], i, j, True).T, own(i), preferred_element_type=jnp.float32
                )
                value = term if value is None else value + term
            add(j, value)

    for n, pair in enumerate(finished):
        update = (sums if pair in begun else inputs)[pair][...]
        obuf[n] = (own(pair).astype(jnp.float32) - 0.5 * update).astype(jnp.bfloat16)
        if job["last"]:
            sent.append(
                pltpu.make_async_copy(obuf.at[n], out.at[tile_rows(pair)], out_sem.at[n])
            )
            sent[-1].start()
    if job["last"]:
        for copy in sent:
            copy.wait()


def stage_kernel(source, target, sem):
    copy = pltpu.make_async_copy(source, target, sem)
    copy.start()
    copy.wait()


def cut_kernel(starts, source, *refs):
    targets, sems = refs[:-1], refs[-1]
    copies = [
        pltpu.make_async_copy(source.at[pl.ds(start, target.shape[0])], target, sems.at[n])
        for n, (start, target) in enumerate(zip(starts, targets))
    ]
    for copy in copies:
        copy.start()
    for copy in copies:
        copy.wait()


def cut_rows(array, ranges, limit=VMEM_LIMIT):
    shapes = [
        jax.ShapeDtypeStruct(((last - first) * ROWS, array.shape[1]), array.dtype)
        for first, last in ranges
    ]
    return pl.pallas_call(
        functools.partial(cut_kernel, tuple(first * ROWS for first, _ in ranges)),
        out_shape=shapes,
        in_specs=[pl.BlockSpec(memory_space=pltpu.HBM)],
        out_specs=[pl.BlockSpec(memory_space=pltpu.VMEM)] * len(shapes),
        scratch_shapes=[pltpu.SemaphoreType.DMA((len(shapes),))],
        compiler_params=pltpu.CompilerParams(vmem_limit_bytes=limit),
        cost_estimate=pl.CostEstimate(
            flops=0, bytes_accessed=sum(4 * shape.size for shape in shapes), transcendentals=0
        ),
    )(array)


def staged(array):
    return pl.pallas_call(
        stage_kernel,
        out_shape=jax.ShapeDtypeStruct(array.shape, array.dtype),
        in_specs=[pl.BlockSpec(memory_space=pl.ANY)],
        out_specs=pl.BlockSpec(memory_space=pltpu.VMEM),
        scratch_shapes=[pltpu.SemaphoreType.DMA],
        compiler_params=pltpu.CompilerParams(vmem_limit_bytes=VMEM_LIMIT),
        cost_estimate=pl.CostEstimate(
            flops=0, bytes_accessed=2 * array.size, transcendentals=0
        ),
    )(array)


def join_kernel(*refs):
    sources, target, sems = refs[:-2], refs[-2], refs[-1]
    copies, at = [], 0
    for n, source in enumerate(sources):
        copies.append(
            pltpu.make_async_copy(source, target.at[pl.ds(at, source.shape[0])], sems.at[n])
        )
        at += source.shape[0]
    for copy in copies:
        copy.start()
    for copy in copies:
        copy.wait()


def joined(arrays):
    rows = sum(array.shape[0] for array in arrays)
    return pl.pallas_call(
        join_kernel,
        out_shape=jax.ShapeDtypeStruct((rows, arrays[0].shape[1]), arrays[0].dtype),
        in_specs=[pl.BlockSpec(memory_space=pl.ANY)] * len(arrays),
        out_specs=pl.BlockSpec(memory_space=pltpu.VMEM),
        scratch_shapes=[pltpu.SemaphoreType.DMA((len(arrays),))],
        compiler_params=pltpu.CompilerParams(vmem_limit_bytes=VMEM_LIMIT),
        cost_estimate=pl.CostEstimate(
            flops=0, bytes_accessed=4 * rows * arrays[0].shape[1], transcendentals=0
        ),
    )(*arrays)


def run_steps(
    taper, pieces, steps, owned, state, finished, stored, rows, members, last, parts=None, begins=()
):
    parts = tuple(range(len(pieces))) if parts is None else parts
    needed = touched_by(steps) | set(finished)
    touched = set()
    for j, first, count in steps:
        near = set(range(first, first + count))
        touched |= near & owned
        if j in owned and near - {j}:
            touched.add(j)
    acc_in = [pair for pair in sorted(touched | set(finished)) if pair in state]
    acc_out = sorted(touched - set(finished))
    arrays, plan = planned(pieces, sorted(set(parts) | {0}), needed)
    writes = []
    if last:
        for array, (pairs, _) in enumerate(stored):
            writes += [(array, n, pair) for n, pair in enumerate(pairs)]
    operands = [taper.T] + arrays + [state[pair] for pair in acc_in] + list(begins)
    earlier = len(operands)
    if last:
        operands += [block for _, block in stored]
    job = dict(
        parts=parts, plan=plan, steps=steps, owned=owned, acc_in=acc_in, acc_out=acc_out,
        finished=finished, arrays=len(arrays), writes=writes, operands=len(operands),
        earlier=earlier,
        last=last,
    )
    inside = pl.BlockSpec(memory_space=pltpu.VMEM)
    specs = [pl.BlockSpec(memory_space=pltpu.SMEM)] + [inside] * (len(operands) - 1)
    products = sum(n for _, _, n in steps)
    count = max(len(finished), 1)
    carries = [jax.ShapeDtypeStruct((ROWS, members), jnp.float32)] * len(acc_out)
    block = (len(finished), ROWS, members)
    scratch = [pltpu.VMEM((count, ROWS, members), jnp.float32)]
    if last:
        shapes = [jax.ShapeDtypeStruct((rows, members), jnp.bfloat16)]
        out_specs = [pl.BlockSpec(memory_space=pl.ANY)]
        scratch += [
            pltpu.VMEM(block, jnp.bfloat16),
            pltpu.SemaphoreType.DMA((len(finished) + len(writes),)),
        ]
    else:
        shapes = [jax.ShapeDtypeStruct(block, jnp.bfloat16)] * int(bool(finished)) + carries
        out_specs = [inside] * len(shapes)
    outputs = pl.pallas_call(
        functools.partial(update_kernel, job),
        out_shape=shapes,
        in_specs=specs,
        out_specs=out_specs,
        scratch_shapes=scratch,
        compiler_params=pltpu.CompilerParams(vmem_limit_bytes=VMEM_LIMIT),
        cost_estimate=pl.CostEstimate(
            flops=2 * products * ROWS * ROWS * members * (len(parts) + 2),
            bytes_accessed=2 * ROWS * members * (len(plan) + 3 * len(finished)),
            transcendentals=0,
        ),
    )(*operands)
    if last:
        return outputs[0], state
    if finished:
        stored.append((finished, outputs[0]))
        outputs = outputs[1:]
    state = {pair: value for pair, value in state.items() if pair not in touched}
    state.update(zip(acc_out, outputs))
    for pair in finished:
        state.pop(pair, None)
    return None, state


def chunk_bounds(pairs):
    first, last = NEAR, pairs - NEAR
    bulk = last - first - 6
    sizes = [2, bulk // 2, bulk - bulk // 2, 2, 2]
    bounds = [first]
    for size in sizes:
        bounds.append(bounds[-1] + size)
    return list(zip(bounds, bounds[1:]))


def per_device(anomalies, taper):
    rows, members = anomalies.shape
    pairs = rows // ROWS
    ring = lax.axis_size("region")
    down = [(i, i + 1) for i in range(ring - 1)]
    up = [(i + 1, i) for i in range(ring - 1)]
    chunks = chunk_bounds(pairs)

    top, bottom, start = cut_rows(
        anomalies, [(0, NEAR), (pairs - NEAR, pairs), chunks[0]], 52 * 2**20
    )
    *cuts, inside = cut_rows(anomalies, chunks[1:] + [(0, pairs)])
    cuts = [start] + cuts
    tops = shifted(top, "member")
    bottoms = shifted(bottom, "member")
    middles = []
    for piece in cuts:
        middles.append(shifted(piece, "member"))

    heads = joined([top] + tops)
    after = lax.ppermute(heads, "region", up)
    tails = joined([bottom] + bottoms)
    before = lax.ppermute(tails, "region", down)

    def run(array, first, count, start=0):
        return {first + n: (array, start + n) for n in range(count)}

    held = [run(inside, 0, pairs)]
    for s in range(len(tops)):
        listed = run(tops[s], 0, NEAR) | run(bottoms[s], pairs - NEAR, NEAR)
        for (first, last), middle in zip(chunks, middles):
            listed |= run(middle[s], first, last - first)
        held.append(listed)
    for n, listed in enumerate(held):
        listed |= run(before, -NEAR, NEAR, n * NEAR) | run(after, pairs, NEAR, n * NEAR)

    pieces = list(held)
    for turn in range(lax.axis_size("tile") - 1):
        sent = {}

        def passed(array):
            if id(array) not in sent:
                if array is inside:
                    moved = shifted(inside, "tile")[turn]
                    sent[id(array)] = staged(moved)
                else:
                    sent[id(array)] = shifted(array, "tile")[turn]
            return sent[id(array)]

        for listed in held:
            pieces.append({pair: (passed(array), n) for pair, (array, n) in listed.items()})

    owned = set(range(pairs))
    state, stored = {}, []

    def steps_for(fresh, before):
        there, steps = set(before), []
        for j in fresh:
            there.add(j)
            near = [i for i in range(j - NEAR, j + NEAR + 1) if i in there and (i in owned or j in owned)]
            while near:
                run = [near[0]]
                while run[-1] + 1 in near:
                    run.append(run[-1] + 1)
                steps.append((j, run[0], len(run)))
                near = near[len(run) :]
        return steps, there

    there, done = set(), set()
    low, high = list(range(NEAR)), list(range(pairs - NEAR, pairs))
    around = list(range(-NEAR, 0)) + list(range(pairs, pairs + NEAR))
    batches = [low + list(range(*chunks[0])), high + around]
    batches += [list(range(*c)) for c in chunks[1:]]
    for n, fresh in enumerate(batches):
        steps, there = steps_for(fresh, there)
        ready = [
            i for i in range(pairs)
            if i not in done and all(k in there for k in range(i - NEAR, i + NEAR + 1))
        ]
        done |= set(ready)
        end = n == len(batches) - 1
        parts, begins = None, ()
        if end and len(pieces) == 2 * len(held):
            near_parts, half = (0, len(held)), tuple(range(1, len(held)))
            parts = tuple(len(held) + part for part in half)
            begins = partial_grams(pieces, near_parts, steps, ())
            begins = partial_grams(pieces, half, steps, begins)
        result, state = run_steps(
            taper, pieces, steps, owned, state, ready, stored, rows, members,
            end, parts, begins,
        )
    return result


def solution(mesh):
    in_specs = (P(("groups", "region"), ("member", "tile")), P(("groups", "region"), None))
    out_specs = P(("groups", "region"), ("member", "tile"))

    return jax.shard_map(
        per_device, mesh=mesh, in_specs=in_specs, out_specs=out_specs, check_vma=False
    )
```

```python
import functools

import jax
import jax.numpy as jnp
from jax import lax
from jax.experimental import pallas as pl
from jax.experimental.pallas import tpu as pltpu
from jax.sharding import PartitionSpec as P


MEMBERS = 1024
BLOCK = 128
REACH = 4
SLOTS = 9
FACTOR = 1.0 / (MEMBERS - 1)
PAIR = 2
ROWS = PAIR * BLOCK
NEAR = REACH // PAIR
VMEM_LIMIT = 24 * 2**20


def shifted(value, axis):
    count = lax.axis_size(axis)
    return [
        lax.ppermute(value, axis, [(i, (i + s) % count) for i in range(count)])
        for s in range(1, count)
    ]


def tile_rows(start, count=1):
    return pl.ds(start * ROWS, count * ROWS)


def gram_rows(held, j, near, begin=None):
    left = jnp.concatenate([held(i) for i in near], axis=0)
    half = left.shape[0] // 2
    halves = []
    for n in range(2):
        part = lax.dot_general(
            left[n * half : (n + 1) * half],
            held(j),
            (((1,), (1,)), ((), ())),
            preferred_element_type=jnp.float32,
        )
        halves.append(part if begin is None else part + begin[pl.ds(n * half, half), :])
    return jnp.concatenate(halves, axis=0)


def partial_kernel(parts, plan, steps, arrays, *refs):
    sources, begins, outs = refs[:arrays], refs[arrays : -len(steps)], refs[-len(steps) :]

    def held(pair):
        pieces = [plan[pair, part] for part in parts]
        return jnp.concatenate([sources[n][tile_rows(start), :] for n, start in pieces], axis=1)

    for k, (j, first, count) in enumerate(steps):
        near = list(range(first, first + count))
        outs[k][...] = gram_rows(held, j, near, begins[k] if begins else None)


def planned(pieces, parts, pairs):
    arrays, plan = [], {}
    for pair in sorted(pairs):
        for part in parts:
            array, start = pieces[part][pair]
            known = [n for n, other in enumerate(arrays) if other is array]
            if not known:
                arrays.append(array)
                known = [len(arrays) - 1]
            plan[pair, part] = (known[0], start)
    return arrays, plan


def touched_by(steps):
    pairs = set()
    for j, first, count in steps:
        pairs |= {j} | set(range(first, first + count))
    return pairs


def partial_grams(pieces, parts, steps, begins):
    arrays, plan = planned(pieces, parts, touched_by(steps))
    inside = pl.BlockSpec(memory_space=pltpu.VMEM)
    products = sum(n for _, _, n in steps)
    members = arrays[0].shape[1]
    return pl.pallas_call(
        functools.partial(partial_kernel, parts, plan, steps, len(arrays)),
        out_shape=[jax.ShapeDtypeStruct((n * ROWS, ROWS), jnp.float32) for _, _, n in steps],
        in_specs=[inside] * (len(arrays) + len(begins)),
        out_specs=[inside] * len(steps),
        compiler_params=pltpu.CompilerParams(vmem_limit_bytes=VMEM_LIMIT),
        cost_estimate=pl.CostEstimate(
            flops=2 * products * ROWS * ROWS * members * len(parts),
            bytes_accessed=4 * products * ROWS * ROWS,
            transcendentals=0,
        ),
    )(*arrays, *begins)


def update_kernel(job, *refs):
    parts = job["parts"]
    plan, steps, owned = job["plan"], job["steps"], job["owned"]
    acc_in, acc_out, finished = job["acc_in"], job["acc_out"], job["finished"]
    writes = job["writes"]
    arrays = job["arrays"]
    taper_source, taper, taper_sem = refs[0], *refs[-2:]
    refs = refs[:-2]
    taper_copy = pltpu.make_async_copy(taper_source, taper, taper_sem)
    taper_copy.start()
    sources = refs[1 : 1 + arrays]
    inputs = dict(zip(acc_in, refs[1 + arrays : 1 + arrays + len(acc_in)]))
    begins = refs[1 + arrays + len(acc_in) : job["earlier"]]
    earlier = refs[job["earlier"] : job["operands"]]
    outs = refs[job["operands"] :]
    if job["last"]:
        out, acc, obuf, out_sem = outs[0], *outs[-3:]
        sent = [
            pltpu.make_async_copy(
                earlier[array].at[n], out.at[tile_rows(pair)], out_sem.at[len(finished) + k]
            )
            for k, (array, n, pair) in enumerate(writes)
        ]
        for copy in sent:
            copy.start()
    else:
        outs, acc = outs[:-1], outs[-1]
        if finished:
            obuf, outs = outs[0], outs[1:]
    carried = outs
    sums = {pair: carried[n] for n, pair in enumerate(acc_out)}
    sums |= {pair: acc.at[n] for n, pair in enumerate(finished)}
    begun = set()

    def piece(pair, part):
        array, start = plan[pair, part]
        return sources[array][tile_rows(start), :]

    def held(pair):
        return jnp.concatenate([piece(pair, part) for part in parts], axis=1)

    def own(pair):
        return piece(pair, 0)

    def add(pair, value):
        if pair in begun:
            value = sums[pair][...] + value
        elif pair in acc_in:
            value = inputs[pair][...] + value
        sums[pair][...] = value
        begun.add(pair)

    def weighted(c, i_pair, j_pair, flip):
        rows = []
        for ii in range(PAIR):
            row = []
            for jj in range(PAIR):
                i, j = i_pair * PAIR + ii, j_pair * PAIR + jj
                slot = (i - j if flip else j - i) + REACH
                if 0 <= slot < SLOTS:
                    weight = taper[slot, j if flip else i] * FACTOR
                    tile = c[ii * BLOCK : (ii + 1) * BLOCK, jj * BLOCK : (jj + 1) * BLOCK]
                    row.append((tile * weight).astype(jnp.bfloat16))
                else:
                    row.append(jnp.zeros((BLOCK, BLOCK), jnp.bfloat16))
            rows.append(jnp.concatenate(row, axis=1))
        return jnp.concatenate(rows, axis=0)

    settled = set()

    def finish(pairs):
        for pair in pairs:
            n = finished.index(pair)
            update = (sums if pair in begun else inputs)[pair][...]
            obuf[n] = (own(pair).astype(jnp.float32) - 0.5 * update).astype(jnp.bfloat16)
            if job["last"]:
                sent.append(
                    pltpu.make_async_copy(obuf.at[n], out.at[tile_rows(pair)], out_sem.at[n])
                )
                sent[-1].start()
            settled.add(pair)

    for k, (j, first, count) in enumerate(steps):
        near = list(range(first, first + count))
        coming = touched_by(steps[k + 1 :])
        ready = [pair for pair in finished if pair in near + [j] and pair not in coming]
        gram = gram_rows(held, j, near, begins[k] if begins else None)
        if k == 0:
            taper_copy.wait()
        tiles = {i: gram[n * ROWS : (n + 1) * ROWS] for n, i in enumerate(near)}
        mine = [i for i in near if i in owned]
        if mine:
            value = jnp.dot(
                jnp.concatenate([weighted(tiles[i], i, j, False) for i in mine], axis=0),
                own(j),
                preferred_element_type=jnp.float32,
            )
            for n, i in enumerate(mine):
                add(i, value[n * ROWS : (n + 1) * ROWS])
        others = [i for i in near if i != j]
        finish([pair for pair in ready if pair != j])
        if j in owned and others:
            value = None
            for i in others:
                term = jnp.dot(
                    weighted(tiles[i], i, j, True).T, own(i), preferred_element_type=jnp.float32
                )
                value = term if value is None else value + term
            add(j, value)
        finish([pair for pair in ready if pair == j])

    finish([pair for pair in finished if pair not in settled])
    if job["last"]:
        for copy in sent:
            copy.wait()


def stage_kernel(source, target, sem):
    copy = pltpu.make_async_copy(source, target, sem)
    copy.start()
    copy.wait()


def cut_kernel(starts, source, *refs):
    targets, sems = refs[:-1], refs[-1]
    copies = [
        pltpu.make_async_copy(source.at[pl.ds(start, target.shape[0])], target, sems.at[n])
        for n, (start, target) in enumerate(zip(starts, targets))
    ]
    for copy in copies:
        copy.start()
    for copy in copies:
        copy.wait()


def cut_rows(array, ranges, limit=VMEM_LIMIT):
    shapes = [
        jax.ShapeDtypeStruct(((last - first) * ROWS, array.shape[1]), array.dtype)
        for first, last in ranges
    ]
    return pl.pallas_call(
        functools.partial(cut_kernel, tuple(first * ROWS for first, _ in ranges)),
        out_shape=shapes,
        in_specs=[pl.BlockSpec(memory_space=pltpu.HBM)],
        out_specs=[pl.BlockSpec(memory_space=pltpu.VMEM)] * len(shapes),
        scratch_shapes=[pltpu.SemaphoreType.DMA((len(shapes),))],
        compiler_params=pltpu.CompilerParams(vmem_limit_bytes=limit),
        cost_estimate=pl.CostEstimate(
            flops=0, bytes_accessed=sum(4 * shape.size for shape in shapes), transcendentals=0
        ),
    )(array)


def staged(array):
    return pl.pallas_call(
        stage_kernel,
        out_shape=jax.ShapeDtypeStruct(array.shape, array.dtype),
        in_specs=[pl.BlockSpec(memory_space=pl.ANY)],
        out_specs=pl.BlockSpec(memory_space=pltpu.VMEM),
        scratch_shapes=[pltpu.SemaphoreType.DMA],
        compiler_params=pltpu.CompilerParams(vmem_limit_bytes=VMEM_LIMIT),
        cost_estimate=pl.CostEstimate(
            flops=0, bytes_accessed=2 * array.size, transcendentals=0
        ),
    )(array)


def join_kernel(*refs):
    sources, target, sems = refs[:-2], refs[-2], refs[-1]
    copies, at = [], 0
    for n, source in enumerate(sources):
        copies.append(
            pltpu.make_async_copy(source, target.at[pl.ds(at, source.shape[0])], sems.at[n])
        )
        at += source.shape[0]
    for copy in copies:
        copy.start()
    for copy in copies:
        copy.wait()


def joined(arrays):
    rows = sum(array.shape[0] for array in arrays)
    return pl.pallas_call(
        join_kernel,
        out_shape=jax.ShapeDtypeStruct((rows, arrays[0].shape[1]), arrays[0].dtype),
        in_specs=[pl.BlockSpec(memory_space=pl.ANY)] * len(arrays),
        out_specs=pl.BlockSpec(memory_space=pltpu.VMEM),
        scratch_shapes=[pltpu.SemaphoreType.DMA((len(arrays),))],
        compiler_params=pltpu.CompilerParams(vmem_limit_bytes=VMEM_LIMIT),
        cost_estimate=pl.CostEstimate(
            flops=0, bytes_accessed=4 * rows * arrays[0].shape[1], transcendentals=0
        ),
    )(*arrays)


def run_steps(
    taper, pieces, steps, owned, state, finished, stored, rows, members, last, parts=None, begins=()
):
    parts = tuple(range(len(pieces))) if parts is None else parts
    needed = touched_by(steps) | set(finished)
    touched = set()
    for j, first, count in steps:
        near = set(range(first, first + count))
        touched |= near & owned
        if j in owned and near - {j}:
            touched.add(j)
    acc_in = [pair for pair in sorted(touched | set(finished)) if pair in state]
    acc_out = sorted(touched - set(finished))
    arrays, plan = planned(pieces, sorted(set(parts) | {0}), needed)
    writes = []
    if last:
        for array, (pairs, _) in enumerate(stored):
            writes += [(array, n, pair) for n, pair in enumerate(pairs)]
    operands = [taper.T] + arrays + [state[pair] for pair in acc_in] + list(begins)
    earlier = len(operands)
    if last:
        operands += [block for _, block in stored]
    job = dict(
        parts=parts, plan=plan, steps=steps, owned=owned, acc_in=acc_in, acc_out=acc_out,
        finished=finished, arrays=len(arrays), writes=writes, operands=len(operands),
        earlier=earlier,
        last=last,
    )
    inside = pl.BlockSpec(memory_space=pltpu.VMEM)
    specs = [inside] * len(operands)
    products = sum(n for _, _, n in steps)
    count = max(len(finished), 1)
    carries = [jax.ShapeDtypeStruct((ROWS, members), jnp.float32)] * len(acc_out)
    block = (len(finished), ROWS, members)
    scratch = [pltpu.VMEM((count, ROWS, members), jnp.float32)]
    if last:
        shapes = [jax.ShapeDtypeStruct((rows, members), jnp.bfloat16)]
        out_specs = [pl.BlockSpec(memory_space=pl.ANY)]
        scratch += [
            pltpu.VMEM(block, jnp.bfloat16),
            pltpu.SemaphoreType.DMA((len(finished) + len(writes),)),
        ]
    else:
        shapes = [jax.ShapeDtypeStruct(block, jnp.bfloat16)] * int(bool(finished)) + carries
        out_specs = [inside] * len(shapes)
    scratch += [pltpu.SMEM(operands[0].shape, jnp.float32), pltpu.SemaphoreType.DMA]
    outputs = pl.pallas_call(
        functools.partial(update_kernel, job),
        out_shape=shapes,
        in_specs=specs,
        out_specs=out_specs,
        scratch_shapes=scratch,
        compiler_params=pltpu.CompilerParams(vmem_limit_bytes=VMEM_LIMIT),
        cost_estimate=pl.CostEstimate(
            flops=2 * products * ROWS * ROWS * members * (len(parts) + 2),
            bytes_accessed=2 * ROWS * members * (len(plan) + 3 * len(finished)),
            transcendentals=0,
        ),
    )(*operands)
    if last:
        return outputs[0], state
    if finished:
        stored.append((finished, outputs[0]))
        outputs = outputs[1:]
    state = {pair: value for pair, value in state.items() if pair not in touched}
    state.update(zip(acc_out, outputs))
    for pair in finished:
        state.pop(pair, None)
    return None, state


def chunk_bounds(pairs):
    first, last = NEAR, pairs - NEAR
    bulk = last - first - 6
    sizes = [2, bulk // 2, bulk - bulk // 2, 2, 2]
    bounds = [first]
    for size in sizes:
        bounds.append(bounds[-1] + size)
    return list(zip(bounds, bounds[1:]))


def per_device(anomalies, taper):
    rows, members = anomalies.shape
    pairs = rows // ROWS
    ring = lax.axis_size("region")
    down = [(i, i + 1) for i in range(ring - 1)]
    up = [(i + 1, i) for i in range(ring - 1)]
    chunks = chunk_bounds(pairs)

    (top,) = cut_rows(anomalies, [(0, NEAR)], 52 * 2**20)
    bottom, start = cut_rows(anomalies, [(pairs - NEAR, pairs), chunks[0]])
    *cuts, inside = cut_rows(anomalies, chunks[1:] + [(0, pairs)])
    cuts = [start] + cuts
    tops = shifted(top, "member")
    bottoms = shifted(bottom, "member")
    middles = []
    for piece in cuts:
        middles.append(shifted(piece, "member"))

    heads = joined([top] + tops)
    after = lax.ppermute(heads, "region", up)
    tails = joined([bottom] + bottoms)
    before = lax.ppermute(tails, "region", down)

    def run(array, first, count, start=0):
        return {first + n: (array, start + n) for n in range(count)}

    held = [run(inside, 0, pairs)]
    for s in range(len(tops)):
        listed = run(tops[s], 0, NEAR) | run(bottoms[s], pairs - NEAR, NEAR)
        for (first, last), middle in zip(chunks, middles):
            listed |= run(middle[s], first, last - first)
        held.append(listed)
    for n, listed in enumerate(held):
        listed |= run(before, -NEAR, NEAR, n * NEAR) | run(after, pairs, NEAR, n * NEAR)

    pieces = list(held)
    for turn in range(lax.axis_size("tile") - 1):
        sent = {}

        def passed(array):
            if id(array) not in sent:
                if array is inside:
                    moved = shifted(inside, "tile")[turn]
                    sent[id(array)] = staged(moved)
                else:
                    sent[id(array)] = shifted(array, "tile")[turn]
            return sent[id(array)]

        for listed in held:
            pieces.append({pair: (passed(array), n) for pair, (array, n) in listed.items()})

    owned = set(range(pairs))
    state, stored = {}, []

    def steps_for(fresh, before):
        there, steps = set(before), []
        for j in fresh:
            there.add(j)
            near = [i for i in range(j - NEAR, j + NEAR + 1) if i in there and (i in owned or j in owned)]
            while near:
                run = [near[0]]
                while run[-1] + 1 in near:
                    run.append(run[-1] + 1)
                steps.append((j, run[0], len(run)))
                near = near[len(run) :]
        return steps, there

    there, done = set(), set()
    low, high = list(range(NEAR)), list(range(pairs - NEAR, pairs))
    around = list(range(-NEAR, 0)) + list(range(pairs, pairs + NEAR))
    batches = [low + list(range(*chunks[0])), high + around]
    batches += [list(range(*c)) for c in chunks[1:]]
    for n, fresh in enumerate(batches):
        steps, there = steps_for(fresh, there)
        ready = [
            i for i in range(pairs)
            if i not in done and all(k in there for k in range(i - NEAR, i + NEAR + 1))
        ]
        done |= set(ready)
        end = n == len(batches) - 1
        parts, begins = None, ()
        if end and len(pieces) == 2 * len(held):
            near_parts, half = (0, len(held)), tuple(range(1, len(held)))
            parts = tuple(len(held) + part for part in half)
            begins = partial_grams(pieces, near_parts, steps, ())
            begins = partial_grams(pieces, half, steps, begins)
        result, state = run_steps(
            taper, pieces, steps, owned, state, ready, stored, rows, members,
            end, parts, begins,
        )
    return result


def solution(mesh):
    in_specs = (P(("groups", "region"), ("member", "tile")), P(("groups", "region"), None))
    out_specs = P(("groups", "region"), ("member", "tile"))

    return jax.shard_map(
        per_device, mesh=mesh, in_specs=in_specs, out_specs=out_specs, check_vma=False
    )
```

```python
import functools

import jax
import jax.numpy as jnp
from jax import lax
from jax.experimental import pallas as pl
from jax.experimental.pallas import tpu as pltpu
from jax.sharding import PartitionSpec as P


MEMBERS = 1024
BLOCK = 128
REACH = 4
SLOTS = 9
FACTOR = 1.0 / (MEMBERS - 1)
PAIR = 2
ROWS = PAIR * BLOCK
NEAR = REACH // PAIR
VMEM_LIMIT = 24 * 2**20


def shifted(value, axis):
    count = lax.axis_size(axis)
    return [
        lax.ppermute(value, axis, [(i, (i + s) % count) for i in range(count)])
        for s in range(1, count)
    ]


def tile_rows(start, count=1):
    return pl.ds(start * ROWS, count * ROWS)


def gram_rows(held, j, near, begin=None):
    left = jnp.concatenate([held(i) for i in near], axis=0)
    half = left.shape[0] // 2
    halves = []
    for n in range(2):
        part = lax.dot_general(
            left[n * half : (n + 1) * half],
            held(j),
            (((1,), (1,)), ((), ())),
            preferred_element_type=jnp.float32,
        )
        halves.append(part if begin is None else part + begin[pl.ds(n * half, half), :])
    return jnp.concatenate(halves, axis=0)


def partial_kernel(parts, plan, steps, arrays, *refs):
    sources, begins, outs = refs[:arrays], refs[arrays : -len(steps)], refs[-len(steps) :]

    def held(pair):
        pieces = [plan[pair, part] for part in parts]
        return jnp.concatenate([sources[n][tile_rows(start), :] for n, start in pieces], axis=1)

    for k, (j, first, count) in enumerate(steps):
        near = list(range(first, first + count))
        outs[k][...] = gram_rows(held, j, near, begins[k] if begins else None)


def planned(pieces, parts, pairs):
    arrays, plan = [], {}
    for pair in sorted(pairs):
        for part in parts:
            array, start = pieces[part][pair]
            known = [n for n, other in enumerate(arrays) if other is array]
            if not known:
                arrays.append(array)
                known = [len(arrays) - 1]
            plan[pair, part] = (known[0], start)
    return arrays, plan


def touched_by(steps):
    pairs = set()
    for j, first, count in steps:
        pairs |= {j} | set(range(first, first + count))
    return pairs


def partial_grams(pieces, parts, steps, begins):
    arrays, plan = planned(pieces, parts, touched_by(steps))
    inside = pl.BlockSpec(memory_space=pltpu.VMEM)
    products = sum(n for _, _, n in steps)
    members = arrays[0].shape[1]
    return pl.pallas_call(
        functools.partial(partial_kernel, parts, plan, steps, len(arrays)),
        out_shape=[jax.ShapeDtypeStruct((n * ROWS, ROWS), jnp.float32) for _, _, n in steps],
        in_specs=[inside] * (len(arrays) + len(begins)),
        out_specs=[inside] * len(steps),
        compiler_params=pltpu.CompilerParams(vmem_limit_bytes=VMEM_LIMIT),
        cost_estimate=pl.CostEstimate(
            flops=2 * products * ROWS * ROWS * members * len(parts),
            bytes_accessed=4 * products * ROWS * ROWS,
            transcendentals=0,
        ),
    )(*arrays, *begins)


def update_kernel(job, *refs):
    parts = job["parts"]
    plan, steps, owned = job["plan"], job["steps"], job["owned"]
    acc_in, acc_out, finished = job["acc_in"], job["acc_out"], job["finished"]
    writes = job["writes"]
    arrays = job["arrays"]
    taper_source, taper, taper_sem = refs[0], *refs[-2:]
    refs = refs[:-2]
    taper_copy = pltpu.make_async_copy(taper_source, taper, taper_sem)
    taper_copy.start()
    sources = refs[1 : 1 + arrays]
    inputs = dict(zip(acc_in, refs[1 + arrays : 1 + arrays + len(acc_in)]))
    begins = refs[1 + arrays + len(acc_in) : job["earlier"]]
    earlier = refs[job["earlier"] : job["operands"]]
    outs = refs[job["operands"] :]
    if job["last"]:
        out, acc, obuf, out_sem = outs[0], *outs[-3:]
        sent = [
            pltpu.make_async_copy(
                earlier[array].at[n], out.at[tile_rows(pair)], out_sem.at[len(finished) + k]
            )
            for k, (array, n, pair) in enumerate(writes)
        ]
        for copy in sent:
            copy.start()
    else:
        outs, acc = outs[:-1], outs[-1]
        if finished:
            obuf, outs = outs[0], outs[1:]
    carried = outs
    sums = {pair: carried[n] for n, pair in enumerate(acc_out)}
    sums |= {pair: acc.at[n] for n, pair in enumerate(finished)}
    begun = set()

    def piece(pair, part):
        array, start = plan[pair, part]
        return sources[array][tile_rows(start), :]

    def held(pair):
        return jnp.concatenate([piece(pair, part) for part in parts], axis=1)

    def own(pair):
        return piece(pair, 0)

    def add(pair, value):
        if pair in begun:
            value = sums[pair][...] + value
        elif pair in acc_in:
            value = inputs[pair][...] + value
        sums[pair][...] = value
        begun.add(pair)

    def weighted(c, i_pair, j_pair, flip):
        rows = []
        for ii in range(PAIR):
            row = []
            for jj in range(PAIR):
                i, j = i_pair * PAIR + ii, j_pair * PAIR + jj
                slot = (i - j if flip else j - i) + REACH
                if 0 <= slot < SLOTS:
                    weight = taper[slot, j if flip else i] * FACTOR
                    tile = c[ii * BLOCK : (ii + 1) * BLOCK, jj * BLOCK : (jj + 1) * BLOCK]
                    row.append((tile * weight).astype(jnp.bfloat16))
                else:
                    row.append(jnp.zeros((BLOCK, BLOCK), jnp.bfloat16))
            rows.append(jnp.concatenate(row, axis=1))
        return jnp.concatenate(rows, axis=0)

    settled = set()

    def finish(pairs):
        for pair in pairs:
            n = finished.index(pair)
            update = (sums if pair in begun else inputs)[pair][...]
            obuf[n] = (own(pair).astype(jnp.float32) - 0.5 * update).astype(jnp.bfloat16)
            if job["last"]:
                sent.append(
                    pltpu.make_async_copy(obuf.at[n], out.at[tile_rows(pair)], out_sem.at[n])
                )
                sent[-1].start()
            settled.add(pair)

    for k, (j, first, count) in enumerate(steps):
        near = list(range(first, first + count))
        coming = touched_by(steps[k + 1 :])
        ready = [pair for pair in finished if pair in near + [j] and pair not in coming]
        gram = gram_rows(held, j, near, begins[k] if begins else None)
        if k == 0:
            taper_copy.wait()
        tiles = {i: gram[n * ROWS : (n + 1) * ROWS] for n, i in enumerate(near)}
        mine = [i for i in near if i in owned]
        if mine:
            value = jnp.dot(
                jnp.concatenate([weighted(tiles[i], i, j, False) for i in mine], axis=0),
                own(j),
                preferred_element_type=jnp.float32,
            )
            for n, i in enumerate(mine):
                add(i, value[n * ROWS : (n + 1) * ROWS])
        others = [i for i in near if i != j]
        finish([pair for pair in ready if pair != j])
        if j in owned and others:
            value = None
            for i in others:
                term = jnp.dot(
                    weighted(tiles[i], i, j, True).T, own(i), preferred_element_type=jnp.float32
                )
                value = term if value is None else value + term
            add(j, value)
        finish([pair for pair in ready if pair == j])

    finish([pair for pair in finished if pair not in settled])
    if job["last"]:
        for copy in sent:
            copy.wait()


def stage_kernel(source, target, sem):
    copy = pltpu.make_async_copy(source, target, sem)
    copy.start()
    copy.wait()


def cut_kernel(starts, source, *refs):
    targets, sems = refs[:-1], refs[-1]
    copies = [
        pltpu.make_async_copy(source.at[pl.ds(start, target.shape[0])], target, sems.at[n])
        for n, (start, target) in enumerate(zip(starts, targets))
    ]
    for copy in copies:
        copy.start()
    for copy in copies:
        copy.wait()


def cut_rows(array, ranges, limit=VMEM_LIMIT):
    shapes = [
        jax.ShapeDtypeStruct(((last - first) * ROWS, array.shape[1]), array.dtype)
        for first, last in ranges
    ]
    return pl.pallas_call(
        functools.partial(cut_kernel, tuple(first * ROWS for first, _ in ranges)),
        out_shape=shapes,
        in_specs=[pl.BlockSpec(memory_space=pltpu.HBM)],
        out_specs=[pl.BlockSpec(memory_space=pltpu.VMEM)] * len(shapes),
        scratch_shapes=[pltpu.SemaphoreType.DMA((len(shapes),))],
        compiler_params=pltpu.CompilerParams(vmem_limit_bytes=limit),
        cost_estimate=pl.CostEstimate(
            flops=0, bytes_accessed=sum(4 * shape.size for shape in shapes), transcendentals=0
        ),
    )(array)


def staged(array):
    return pl.pallas_call(
        stage_kernel,
        out_shape=jax.ShapeDtypeStruct(array.shape, array.dtype),
        in_specs=[pl.BlockSpec(memory_space=pl.ANY)],
        out_specs=pl.BlockSpec(memory_space=pltpu.VMEM),
        scratch_shapes=[pltpu.SemaphoreType.DMA],
        compiler_params=pltpu.CompilerParams(vmem_limit_bytes=VMEM_LIMIT),
        cost_estimate=pl.CostEstimate(
            flops=0, bytes_accessed=2 * array.size, transcendentals=0
        ),
    )(array)


def join_kernel(*refs):
    sources, target, sems = refs[:-2], refs[-2], refs[-1]
    copies, at = [], 0
    for n, source in enumerate(sources):
        copies.append(
            pltpu.make_async_copy(source, target.at[pl.ds(at, source.shape[0])], sems.at[n])
        )
        at += source.shape[0]
    for copy in copies:
        copy.start()
    for copy in copies:
        copy.wait()


def joined(arrays):
    rows = sum(array.shape[0] for array in arrays)
    return pl.pallas_call(
        join_kernel,
        out_shape=jax.ShapeDtypeStruct((rows, arrays[0].shape[1]), arrays[0].dtype),
        in_specs=[pl.BlockSpec(memory_space=pl.ANY)] * len(arrays),
        out_specs=pl.BlockSpec(memory_space=pltpu.VMEM),
        scratch_shapes=[pltpu.SemaphoreType.DMA((len(arrays),))],
        compiler_params=pltpu.CompilerParams(vmem_limit_bytes=VMEM_LIMIT),
        cost_estimate=pl.CostEstimate(
            flops=0, bytes_accessed=4 * rows * arrays[0].shape[1], transcendentals=0
        ),
    )(*arrays)


def run_steps(
    taper, pieces, steps, owned, state, finished, stored, rows, members, last, parts=None, begins=()
):
    parts = tuple(range(len(pieces))) if parts is None else parts
    needed = touched_by(steps) | set(finished)
    touched = set()
    for j, first, count in steps:
        near = set(range(first, first + count))
        touched |= near & owned
        if j in owned and near - {j}:
            touched.add(j)
    acc_in = [pair for pair in sorted(touched | set(finished)) if pair in state]
    acc_out = sorted(touched - set(finished))
    arrays, plan = planned(pieces, sorted(set(parts) | {0}), needed)
    writes = []
    if last:
        for array, (pairs, _) in enumerate(stored):
            writes += [(array, n, pair) for n, pair in enumerate(pairs)]
    operands = [taper.T] + arrays + [state[pair] for pair in acc_in] + list(begins)
    earlier = len(operands)
    if last:
        operands += [block for _, block in stored]
    job = dict(
        parts=parts, plan=plan, steps=steps, owned=owned, acc_in=acc_in, acc_out=acc_out,
        finished=finished, arrays=len(arrays), writes=writes, operands=len(operands),
        earlier=earlier,
        last=last,
    )
    inside = pl.BlockSpec(memory_space=pltpu.VMEM)
    specs = [inside] * len(operands)
    products = sum(n for _, _, n in steps)
    count = max(len(finished), 1)
    carries = [jax.ShapeDtypeStruct((ROWS, members), jnp.float32)] * len(acc_out)
    block = (len(finished), ROWS, members)
    scratch = [pltpu.VMEM((count, ROWS, members), jnp.float32)]
    if last:
        shapes = [jax.ShapeDtypeStruct((rows, members), jnp.bfloat16)]
        out_specs = [pl.BlockSpec(memory_space=pl.ANY)]
        scratch += [
            pltpu.VMEM(block, jnp.bfloat16),
            pltpu.SemaphoreType.DMA((len(finished) + len(writes),)),
        ]
    else:
        shapes = [jax.ShapeDtypeStruct(block, jnp.bfloat16)] * int(bool(finished)) + carries
        out_specs = [inside] * len(shapes)
    scratch += [pltpu.SMEM(operands[0].shape, jnp.float32), pltpu.SemaphoreType.DMA]
    outputs = pl.pallas_call(
        functools.partial(update_kernel, job),
        out_shape=shapes,
        in_specs=specs,
        out_specs=out_specs,
        scratch_shapes=scratch,
        compiler_params=pltpu.CompilerParams(vmem_limit_bytes=VMEM_LIMIT),
        cost_estimate=pl.CostEstimate(
            flops=2 * products * ROWS * ROWS * members * (len(parts) + 2),
            bytes_accessed=2 * ROWS * members * (len(plan) + 3 * len(finished)),
            transcendentals=0,
        ),
    )(*operands)
    if last:
        return outputs[0], state
    if finished:
        stored.append((finished, outputs[0]))
        outputs = outputs[1:]
    state = {pair: value for pair, value in state.items() if pair not in touched}
    state.update(zip(acc_out, outputs))
    for pair in finished:
        state.pop(pair, None)
    return None, state


def chunk_bounds(pairs):
    first, last = NEAR, pairs - NEAR
    bulk = last - first - 6
    sizes = [2, bulk // 2, bulk - bulk // 2, 2, 1, 1]
    bounds = [first]
    for size in sizes:
        bounds.append(bounds[-1] + size)
    return list(zip(bounds, bounds[1:]))


def per_device(anomalies, taper):
    rows, members = anomalies.shape
    pairs = rows // ROWS
    ring = lax.axis_size("region")
    down = [(i, i + 1) for i in range(ring - 1)]
    up = [(i + 1, i) for i in range(ring - 1)]
    chunks = chunk_bounds(pairs)

    (top,) = cut_rows(anomalies, [(0, NEAR)], 52 * 2**20)
    bottom, start = cut_rows(anomalies, [(pairs - NEAR, pairs), chunks[0]])
    *cuts, inside = cut_rows(anomalies, chunks[1:] + [(0, pairs)])
    cuts = [start] + cuts
    tops = shifted(top, "member")
    bottoms = shifted(bottom, "member")
    middles = []
    for piece in cuts:
        middles.append(shifted(piece, "member"))

    heads = joined([top] + tops)
    after = lax.ppermute(heads, "region", up)
    tails = joined([bottom] + bottoms)
    before = lax.ppermute(tails, "region", down)

    def run(array, first, count, start=0):
        return {first + n: (array, start + n) for n in range(count)}

    held = [run(inside, 0, pairs)]
    for s in range(len(tops)):
        listed = run(tops[s], 0, NEAR) | run(bottoms[s], pairs - NEAR, NEAR)
        for (first, last), middle in zip(chunks, middles):
            listed |= run(middle[s], first, last - first)
        held.append(listed)
    for n, listed in enumerate(held):
        listed |= run(before, -NEAR, NEAR, n * NEAR) | run(after, pairs, NEAR, n * NEAR)

    pieces = list(held)
    for turn in range(lax.axis_size("tile") - 1):
        sent = {}

        def passed(array):
            if id(array) not in sent:
                if array is inside:
                    moved = shifted(inside, "tile")[turn]
                    sent[id(array)] = staged(moved)
                else:
                    sent[id(array)] = shifted(array, "tile")[turn]
            return sent[id(array)]

        for listed in held:
            pieces.append({pair: (passed(array), n) for pair, (array, n) in listed.items()})

    owned = set(range(pairs))
    state, stored = {}, []

    def steps_for(fresh, before):
        there, steps = set(before), []
        for j in fresh:
            there.add(j)
            near = [i for i in range(j - NEAR, j + NEAR + 1) if i in there and (i in owned or j in owned)]
            while near:
                run = [near[0]]
                while run[-1] + 1 in near:
                    run.append(run[-1] + 1)
                steps.append((j, run[0], len(run)))
                near = near[len(run) :]
        return steps, there

    there, done = set(), set()
    low, high = list(range(NEAR)), list(range(pairs - NEAR, pairs))
    around = list(range(-NEAR, 0)) + list(range(pairs, pairs + NEAR))
    batches = [low + list(range(*chunks[0])), high + around]
    batches += [list(range(*c)) for c in chunks[1:]]
    work = []
    for fresh in batches:
        steps, there = steps_for(fresh, there)
        ready = [
            i for i in range(pairs)
            if i not in done and all(k in there for k in range(i - NEAR, i + NEAR + 1))
        ]
        done |= set(ready)
        work.append((steps, ready))

    tails = len(batches) - 2
    split = len(pieces) == 2 * len(held)
    received = tuple(range(1, len(held)))
    if split:
        sums = partial_grams(
            pieces, (0, len(held)), work[tails][0] + work[tails + 1][0], ()
        )
    for n, (steps, ready) in enumerate(work):
        parts, begins = None, ()
        if split and n >= tails:
            parts = tuple(len(held) + part for part in received)
            begins, sums = sums[: len(steps)], sums[len(steps) :]
            begins = partial_grams(pieces, received, steps, begins)
        result, state = run_steps(
            taper, pieces, steps, owned, state, ready, stored, rows, members,
            n == len(work) - 1, parts, begins,
        )
    return result


def solution(mesh):
    in_specs = (P(("groups", "region"), ("member", "tile")), P(("groups", "region"), None))
    out_specs = P(("groups", "region"), ("member", "tile"))

    return jax.shard_map(
        per_device, mesh=mesh, in_specs=in_specs, out_specs=out_specs, check_vma=False
    )
```

```python
import functools

import jax
import jax.numpy as jnp
from jax import lax
from jax.experimental import pallas as pl
from jax.experimental.pallas import tpu as pltpu
from jax.sharding import PartitionSpec as P


MEMBERS = 1024
BLOCK = 128
REACH = 4
SLOTS = 9
FACTOR = 1.0 / (MEMBERS - 1)
PAIR = 2
ROWS = PAIR * BLOCK
NEAR = REACH // PAIR
VMEM_LIMIT = 24 * 2**20


def shifted(value, axis):
    count = lax.axis_size(axis)
    return [
        lax.ppermute(value, axis, [(i, (i + s) % count) for i in range(count)])
        for s in range(1, count)
    ]


def tile_rows(start, count=1):
    return pl.ds(start * ROWS, count * ROWS)


def gram_rows(held, j, near, begin=None):
    left = jnp.concatenate([held(i) for i in near], axis=0)
    half = left.shape[0] // 2
    halves = []
    for n in range(2):
        part = lax.dot_general(
            left[n * half : (n + 1) * half],
            held(j),
            (((1,), (1,)), ((), ())),
            preferred_element_type=jnp.float32,
        )
        halves.append(part if begin is None else part + begin[pl.ds(n * half, half), :])
    return jnp.concatenate(halves, axis=0)


def partial_kernel(parts, plan, steps, arrays, *refs):
    sources, begins, outs = refs[:arrays], refs[arrays : -len(steps)], refs[-len(steps) :]

    def held(pair):
        pieces = [plan[pair, part] for part in parts]
        return jnp.concatenate([sources[n][tile_rows(start), :] for n, start in pieces], axis=1)

    for k, (j, first, count) in enumerate(steps):
        near = list(range(first, first + count))
        outs[k][...] = gram_rows(held, j, near, begins[k] if begins else None)


def planned(pieces, parts, pairs):
    arrays, plan = [], {}
    for pair in sorted(pairs):
        for part in parts:
            array, start = pieces[part][pair]
            known = [n for n, other in enumerate(arrays) if other is array]
            if not known:
                arrays.append(array)
                known = [len(arrays) - 1]
            plan[pair, part] = (known[0], start)
    return arrays, plan


def touched_by(steps):
    pairs = set()
    for j, first, count in steps:
        pairs |= {j} | set(range(first, first + count))
    return pairs


def partial_grams(pieces, parts, steps, begins):
    arrays, plan = planned(pieces, parts, touched_by(steps))
    inside = pl.BlockSpec(memory_space=pltpu.VMEM)
    products = sum(n for _, _, n in steps)
    members = arrays[0].shape[1]
    return pl.pallas_call(
        functools.partial(partial_kernel, parts, plan, steps, len(arrays)),
        out_shape=[jax.ShapeDtypeStruct((n * ROWS, ROWS), jnp.float32) for _, _, n in steps],
        in_specs=[inside] * (len(arrays) + len(begins)),
        out_specs=[inside] * len(steps),
        compiler_params=pltpu.CompilerParams(vmem_limit_bytes=VMEM_LIMIT),
        cost_estimate=pl.CostEstimate(
            flops=2 * products * ROWS * ROWS * members * len(parts),
            bytes_accessed=4 * products * ROWS * ROWS,
            transcendentals=0,
        ),
    )(*arrays, *begins)


def update_kernel(job, *refs):
    parts = job["parts"]
    plan, steps, owned = job["plan"], job["steps"], job["owned"]
    acc_in, acc_out, finished = job["acc_in"], job["acc_out"], job["finished"]
    writes = job["writes"]
    arrays = job["arrays"]
    taper_source, taper, taper_sem = refs[0], *refs[-2:]
    refs = refs[:-2]
    taper_copy = pltpu.make_async_copy(taper_source, taper, taper_sem)
    taper_copy.start()
    sources = refs[1 : 1 + arrays]
    inputs = dict(zip(acc_in, refs[1 + arrays : 1 + arrays + len(acc_in)]))
    begins = refs[1 + arrays + len(acc_in) : job["earlier"]]
    earlier = refs[job["earlier"] : job["operands"]]
    outs = refs[job["operands"] :]
    sent = []
    if job["writer"]:
        out, outs, out_sem = outs[0], outs[1:-1], outs[-1]
        sent = [
            pltpu.make_async_copy(
                earlier[array].at[n], out.at[tile_rows(pair)], out_sem.at[len(finished) + k]
            )
            for k, (array, n, pair) in enumerate(writes)
        ]
        for copy in sent:
            copy.start()
    if job["last"]:
        obuf, outs = outs[-1], outs[:-1]
    acc, outs = outs[-1], outs[:-1]
    if finished and not job["last"]:
        obuf, outs = outs[0], outs[1:]
    carried = outs
    sums = {pair: carried[n] for n, pair in enumerate(acc_out)}
    sums |= {pair: acc.at[n] for n, pair in enumerate(finished)}
    begun = set()

    def piece(pair, part):
        array, start = plan[pair, part]
        return sources[array][tile_rows(start), :]

    def held(pair):
        return jnp.concatenate([piece(pair, part) for part in parts], axis=1)

    def own(pair):
        return piece(pair, 0)

    def add(pair, value):
        if pair in begun:
            value = sums[pair][...] + value
        elif pair in acc_in:
            value = inputs[pair][...] + value
        sums[pair][...] = value
        begun.add(pair)

    def weighted(c, i_pair, j_pair, flip):
        rows = []
        for ii in range(PAIR):
            row = []
            for jj in range(PAIR):
                i, j = i_pair * PAIR + ii, j_pair * PAIR + jj
                slot = (i - j if flip else j - i) + REACH
                if 0 <= slot < SLOTS:
                    weight = taper[slot, j if flip else i] * FACTOR
                    tile = c[ii * BLOCK : (ii + 1) * BLOCK, jj * BLOCK : (jj + 1) * BLOCK]
                    row.append((tile * weight).astype(jnp.bfloat16))
                else:
                    row.append(jnp.zeros((BLOCK, BLOCK), jnp.bfloat16))
            rows.append(jnp.concatenate(row, axis=1))
        return jnp.concatenate(rows, axis=0)

    settled = set()

    def finish(pairs):
        for pair in pairs:
            n = finished.index(pair)
            update = (sums if pair in begun else inputs)[pair][...]
            obuf[n] = (own(pair).astype(jnp.float32) - 0.5 * update).astype(jnp.bfloat16)
            if job["last"]:
                sent.append(
                    pltpu.make_async_copy(obuf.at[n], out.at[tile_rows(pair)], out_sem.at[n])
                )
                sent[-1].start()
            settled.add(pair)

    for k, (j, first, count) in enumerate(steps):
        near = list(range(first, first + count))
        coming = touched_by(steps[k + 1 :])
        ready = [pair for pair in finished if pair in near + [j] and pair not in coming]
        gram = gram_rows(held, j, near, begins[k] if begins else None)
        if k == 0:
            taper_copy.wait()
        tiles = {i: gram[n * ROWS : (n + 1) * ROWS] for n, i in enumerate(near)}
        mine = [i for i in near if i in owned]
        if mine:
            value = jnp.dot(
                jnp.concatenate([weighted(tiles[i], i, j, False) for i in mine], axis=0),
                own(j),
                preferred_element_type=jnp.float32,
            )
            for n, i in enumerate(mine):
                add(i, value[n * ROWS : (n + 1) * ROWS])
        others = [i for i in near if i != j]
        finish([pair for pair in ready if pair != j])
        if j in owned and others:
            value = None
            for i in others:
                term = jnp.dot(
                    weighted(tiles[i], i, j, True).T, own(i), preferred_element_type=jnp.float32
                )
                value = term if value is None else value + term
            add(j, value)
        finish([pair for pair in ready if pair == j])

    finish([pair for pair in finished if pair not in settled])
    for copy in sent:
        copy.wait()


def stage_kernel(source, target, sem):
    copy = pltpu.make_async_copy(source, target, sem)
    copy.start()
    copy.wait()


def cut_kernel(starts, source, *refs):
    targets, sems = refs[:-1], refs[-1]
    copies = [
        pltpu.make_async_copy(source.at[pl.ds(start, target.shape[0])], target, sems.at[n])
        for n, (start, target) in enumerate(zip(starts, targets))
    ]
    for copy in copies:
        copy.start()
    for copy in copies:
        copy.wait()


def cut_rows(array, ranges, limit=VMEM_LIMIT):
    shapes = [
        jax.ShapeDtypeStruct(((last - first) * ROWS, array.shape[1]), array.dtype)
        for first, last in ranges
    ]
    return pl.pallas_call(
        functools.partial(cut_kernel, tuple(first * ROWS for first, _ in ranges)),
        out_shape=shapes,
        in_specs=[pl.BlockSpec(memory_space=pltpu.HBM)],
        out_specs=[pl.BlockSpec(memory_space=pltpu.VMEM)] * len(shapes),
        scratch_shapes=[pltpu.SemaphoreType.DMA((len(shapes),))],
        compiler_params=pltpu.CompilerParams(vmem_limit_bytes=limit),
        cost_estimate=pl.CostEstimate(
            flops=0, bytes_accessed=sum(4 * shape.size for shape in shapes), transcendentals=0
        ),
    )(array)


def staged(array):
    return pl.pallas_call(
        stage_kernel,
        out_shape=jax.ShapeDtypeStruct(array.shape, array.dtype),
        in_specs=[pl.BlockSpec(memory_space=pl.ANY)],
        out_specs=pl.BlockSpec(memory_space=pltpu.VMEM),
        scratch_shapes=[pltpu.SemaphoreType.DMA],
        compiler_params=pltpu.CompilerParams(vmem_limit_bytes=VMEM_LIMIT),
        cost_estimate=pl.CostEstimate(
            flops=0, bytes_accessed=2 * array.size, transcendentals=0
        ),
    )(array)


def join_kernel(*refs):
    sources, target, sems = refs[:-2], refs[-2], refs[-1]
    copies, at = [], 0
    for n, source in enumerate(sources):
        copies.append(
            pltpu.make_async_copy(source, target.at[pl.ds(at, source.shape[0])], sems.at[n])
        )
        at += source.shape[0]
    for copy in copies:
        copy.start()
    for copy in copies:
        copy.wait()


def joined(arrays):
    rows = sum(array.shape[0] for array in arrays)
    return pl.pallas_call(
        join_kernel,
        out_shape=jax.ShapeDtypeStruct((rows, arrays[0].shape[1]), arrays[0].dtype),
        in_specs=[pl.BlockSpec(memory_space=pl.ANY)] * len(arrays),
        out_specs=pl.BlockSpec(memory_space=pltpu.VMEM),
        scratch_shapes=[pltpu.SemaphoreType.DMA((len(arrays),))],
        compiler_params=pltpu.CompilerParams(vmem_limit_bytes=VMEM_LIMIT),
        cost_estimate=pl.CostEstimate(
            flops=0, bytes_accessed=4 * rows * arrays[0].shape[1], transcendentals=0
        ),
    )(*arrays)


def run_steps(
    taper, pieces, steps, owned, state, finished, stored, rows, members, last, parts=None, begins=(),
    writer=False, result=None,
):
    parts = tuple(range(len(pieces))) if parts is None else parts
    needed = touched_by(steps) | set(finished)
    touched = set()
    for j, first, count in steps:
        near = set(range(first, first + count))
        touched |= near & owned
        if j in owned and near - {j}:
            touched.add(j)
    acc_in = [pair for pair in sorted(touched | set(finished)) if pair in state]
    acc_out = sorted(touched - set(finished))
    arrays, plan = planned(pieces, sorted(set(parts) | {0}), needed)
    writes = []
    writer = writer or last
    if writer:
        for array, (pairs, _) in enumerate(stored):
            writes += [(array, n, pair) for n, pair in enumerate(pairs)]
    operands = [taper.T] + arrays + [state[pair] for pair in acc_in] + list(begins)
    earlier = len(operands)
    aliases = {}
    if writer:
        operands += [block for _, block in stored]
        stored.clear()
        if result is not None:
            aliases = {len(operands): 0}
            operands.append(result)
    job = dict(
        parts=parts, plan=plan, steps=steps, owned=owned, acc_in=acc_in, acc_out=acc_out,
        finished=finished, arrays=len(arrays), writes=writes, operands=len(operands),
        earlier=earlier,
        last=last, writer=writer,
    )
    inside = pl.BlockSpec(memory_space=pltpu.VMEM)
    specs = [pl.BlockSpec(memory_space=pl.ANY) if n in aliases else inside for n in range(len(operands))]
    products = sum(n for _, _, n in steps)
    count = max(len(finished), 1)
    carries = [jax.ShapeDtypeStruct((ROWS, members), jnp.float32)] * len(acc_out)
    block = (len(finished), ROWS, members)
    scratch = [pltpu.VMEM((count, ROWS, members), jnp.float32)]
    shapes, out_specs = [], []
    if writer:
        shapes.append(jax.ShapeDtypeStruct((rows, members), jnp.bfloat16))
        out_specs.append(pl.BlockSpec(memory_space=pl.ANY))
    if last:
        scratch.append(pltpu.VMEM(block, jnp.bfloat16))
    else:
        held_here = [jax.ShapeDtypeStruct(block, jnp.bfloat16)] * int(bool(finished)) + carries
        shapes += held_here
        out_specs += [inside] * len(held_here)
    if writer:
        scratch.append(pltpu.SemaphoreType.DMA((len(finished) + len(writes),)))
    scratch += [pltpu.SMEM(operands[0].shape, jnp.float32), pltpu.SemaphoreType.DMA]
    outputs = pl.pallas_call(
        functools.partial(update_kernel, job),
        out_shape=shapes,
        in_specs=specs,
        out_specs=out_specs,
        scratch_shapes=scratch,
        input_output_aliases=aliases,
        compiler_params=pltpu.CompilerParams(vmem_limit_bytes=VMEM_LIMIT),
        cost_estimate=pl.CostEstimate(
            flops=2 * products * ROWS * ROWS * members * (len(parts) + 2),
            bytes_accessed=2 * ROWS * members * (len(plan) + 3 * len(finished)),
            transcendentals=0,
        ),
    )(*operands)
    if writer:
        result, outputs = outputs[0], outputs[1:]
    if last:
        return result, state
    if finished:
        stored.append((finished, outputs[0]))
        outputs = outputs[1:]
    state = {pair: value for pair, value in state.items() if pair not in touched}
    state.update(zip(acc_out, outputs))
    for pair in finished:
        state.pop(pair, None)
    return result, state


def chunk_bounds(pairs):
    first, last = NEAR, pairs - NEAR
    bulk = last - first - 6
    sizes = [2, bulk // 2, bulk - bulk // 2, 2, 2]
    bounds = [first]
    for size in sizes:
        bounds.append(bounds[-1] + size)
    return list(zip(bounds, bounds[1:]))


def per_device(anomalies, taper):
    rows, members = anomalies.shape
    pairs = rows // ROWS
    ring = lax.axis_size("region")
    down = [(i, i + 1) for i in range(ring - 1)]
    up = [(i + 1, i) for i in range(ring - 1)]
    chunks = chunk_bounds(pairs)

    (top,) = cut_rows(anomalies, [(0, NEAR)], 52 * 2**20)
    bottom, start = cut_rows(anomalies, [(pairs - NEAR, pairs), chunks[0]])
    *cuts, inside = cut_rows(anomalies, chunks[1:] + [(0, pairs)])
    cuts = [start] + cuts
    tops = shifted(top, "member")
    bottoms = shifted(bottom, "member")
    middles = []
    for piece in cuts:
        middles.append(shifted(piece, "member"))

    heads = joined([top] + tops)
    after = lax.ppermute(heads, "region", up)
    tails = joined([bottom] + bottoms)
    before = lax.ppermute(tails, "region", down)

    def run(array, first, count, start=0):
        return {first + n: (array, start + n) for n in range(count)}

    held = [run(inside, 0, pairs)]
    for s in range(len(tops)):
        listed = run(tops[s], 0, NEAR) | run(bottoms[s], pairs - NEAR, NEAR)
        for (first, last), middle in zip(chunks, middles):
            listed |= run(middle[s], first, last - first)
        held.append(listed)
    for n, listed in enumerate(held):
        listed |= run(before, -NEAR, NEAR, n * NEAR) | run(after, pairs, NEAR, n * NEAR)

    pieces = list(held)
    for turn in range(lax.axis_size("tile") - 1):
        sent = {}

        def passed(array):
            if id(array) not in sent:
                if array is inside:
                    moved = shifted(inside, "tile")[turn]
                    sent[id(array)] = staged(moved)
                else:
                    sent[id(array)] = shifted(array, "tile")[turn]
            return sent[id(array)]

        for listed in held:
            pieces.append({pair: (passed(array), n) for pair, (array, n) in listed.items()})

    owned = set(range(pairs))
    state, stored, result = {}, [], None

    def steps_for(fresh, before):
        there, steps = set(before), []
        for j in fresh:
            there.add(j)
            near = [i for i in range(j - NEAR, j + NEAR + 1) if i in there and (i in owned or j in owned)]
            while near:
                run = [near[0]]
                while run[-1] + 1 in near:
                    run.append(run[-1] + 1)
                steps.append((j, run[0], len(run)))
                near = near[len(run) :]
        return steps, there

    there, done = set(), set()
    low, high = list(range(NEAR)), list(range(pairs - NEAR, pairs))
    around = list(range(-NEAR, 0)) + list(range(pairs, pairs + NEAR))
    batches = [low + list(range(*chunks[0])), high + around]
    batches += [list(range(*c)) for c in chunks[1:]]
    for n, fresh in enumerate(batches):
        steps, there = steps_for(fresh, there)
        ready = [
            i for i in range(pairs)
            if i not in done and all(k in there for k in range(i - NEAR, i + NEAR + 1))
        ]
        done |= set(ready)
        end = n == len(batches) - 1
        parts, begins = None, ()
        if end and len(pieces) == 2 * len(held):
            near_parts, half = (0, len(held)), tuple(range(1, len(held)))
            parts = tuple(len(held) + part for part in half)
            begins = partial_grams(pieces, near_parts, steps, ())
            begins = partial_grams(pieces, half, steps, begins)
        result, state = run_steps(
            taper, pieces, steps, owned, state, ready, stored, rows, members,
            end, parts, begins, n >= len(batches) - 3, result,
        )
    return result


def solution(mesh):
    in_specs = (P(("groups", "region"), ("member", "tile")), P(("groups", "region"), None))
    out_specs = P(("groups", "region"), ("member", "tile"))

    return jax.shard_map(
        per_device, mesh=mesh, in_specs=in_specs, out_specs=out_specs, check_vma=False
    )
```
